128 devices in a mesh: grp: 4 (over y), dev: 32 (over x, z, core).
Axes of the slice: x: 4, y: 4, z: 4, core: 2. Of those that a mesh axis runs over, the one named last changes fastest.
Arguments:
- child_weights: float32 [2, 1024, 4, 64, 256], P(None, ('grp', 'dev')), may hold values from -0.12 to 0.12
- pivots: int32 [1024, 32], P(('grp', 'dev')), may hold values from 0 to 1023, as said below
- ranks: int32 [1024], replicated, may hold values from 1 to 32, 10240 in all
- owner_slot: int32 [1024], replicated, may hold values from 0 to 1023, each once
Outputs:
- skeleton_sums: float32 [2, 32, 1024, 256], P(None, None, ('grp', 'dev'))
The draws below stay inside these ranges and needn't reach their ends.
Inputs may be any that keep to these rules, and one draw needn't show every extreme that they name: `pivots`: each row lists 32 distinct points of one target box, numbered row by row within the box. The ranks sum to 10240; some box has rank 32. A permutation: box a is owned by device floor(owner_slot[a] / 8) of grp+dev, at place owner_slot[a] mod 8.
All inputs are finite; a program needn't handle non-finite values.
Results may differ from the reference program's by a relative error of at most 0.0003.
Values sent between devices are 32-bit elements; how exact they have to be, the bound alone decides.
No kernel may reach another device: no remote copies, remote signals or barrier semaphores. Data moves between devices by JAX's collectives and lax.ppermute only.
A program may use at most 64 MiB of HBM per device.

```python
import math
import jax
import jax.numpy as jnp
import numpy as np
from jax import lax

GRID = 2048
Q = 8
R = 64
RT = 32
RMEAN = 10
NSB = 1024
NA = 1024
NAP = 256
NP = 256


def draw_pivots(key, part):
    points = GRID * GRID // 4096
    key_scores, key_high, key_low = jax.random.split(key, 3)
    scores = jax.random.randint(key_scores, (NA, points), 0, 1 << 20, dtype=jnp.int32) * points + jnp.arange(points, dtype=jnp.int32)[None, :]
    high_box = jax.random.randint(key_high, (), 0, NA, dtype=jnp.int32)
    low_box = jax.random.randint(key_low, (), 0, NA, dtype=jnp.int32)
    row_ids = jnp.arange(NA, dtype=jnp.int32)[:, None]
    col_ids = jnp.arange(points, dtype=jnp.int32)[None, :]
    scores = jnp.where((row_ids == high_box) & (col_ids == points - 1), -2, scores)
    scores = jnp.where((row_ids == low_box) & (col_ids == 0), -1, scores)
    ranked = jnp.argsort(scores, axis=1, stable=True)
    return ranked[:, :RT].astype(jnp.int32)


def block_levels(rng, shape, cuts, least, largest):
    def one(position, parts):
        heights = jax.random.uniform(jax.random.fold_in(jax.random.fold_in(rng, 6), position), (parts,), jnp.float32, least / len(cuts), largest / len(cuts))
        return jnp.repeat(jnp.exp(heights), shape[position] // parts).reshape((-1,) + (1,) * (len(shape) - position - 1))

    factor_of = one(*cuts[0])
    for cut in cuts[1:]:
        factor_of = factor_of * one(*cut)
    return factor_of


def length_profile(count, total, most, lean):
    portions = [(1 << 20) // math.isqrt(grade ** lean) + 1 for grade in range(2, count + 1)]
    spare, holding = total - most - (count - 1), [1] * (count - 1)
    while spare > 0:
        candidates = [i for i in range(count - 1) if holding[i] < most]
        whole, left = sum([portions[i] for i in candidates]), spare
        for i in candidates:
            more = min(most - holding[i], max(1, left * portions[i] // whole), spare)
            holding[i] = holding[i] + more
            spare = spare - more
    return np.array([most] + holding)


def ragged_sizes(own_key, amount, total, reach, lean):
    if amount == 2:
        one = jax.random.randint(own_key, (), max(1, total - reach), min(reach, total - 1) + 1)
        return jnp.stack([one, total - one])
    lengths = jnp.asarray(length_profile(amount, total, reach, lean), jnp.int32)
    pairs = (amount - 1) // 2
    donor, taker = lengths[1:1 + 2 * pairs:2], lengths[2:2 + 2 * pairs:2]
    room = jnp.minimum(donor - 1, reach - taker)
    shifted = jax.random.randint(jax.random.fold_in(own_key, 1), (pairs,), 0, 1 << 20) % (room + 1)
    lengths = lengths.at[1:1 + 2 * pairs:2].set(donor - shifted).at[2:2 + 2 * pairs:2].set(taker + shifted)
    return lengths[jax.random.permutation(jax.random.fold_in(own_key, 2), amount)]


def centred(stream_key, shape, scale, limit, cuts=(), held_as=jnp.bfloat16):
    values = scale * jax.random.normal(stream_key, shape, jnp.float32)
    if cuts:
        values = values * block_levels(stream_key, shape, cuts, -0.22, 0.18)
    return jnp.clip(values, -limit, limit).astype(held_as)


def setup_inputs(seed: int = 0) -> dict:
    keys = jax.random.split(jax.random.key(seed), 5)
    return {
        "child_weights": centred(keys[0], (2, NSB, 4, R, NAP), 0.02, 0.12, ((1, 128),), jnp.float32),
        "pivots": draw_pivots(jax.random.fold_in(keys[4], 71), 0),
        "ranks": ragged_sizes(keys[2], NA, NA * RMEAN, RT, 2).astype(jnp.int32),
        "owner_slot": jax.random.permutation(keys[3], NA).astype(jnp.int32),
    }


TWO_PI = 2.0 * math.pi
speed_waves = 8

def cheb_nodes(degree):
    steps_j = jnp.arange(degree, dtype=jnp.float32)
    return jnp.cos(math.pi * (2.0 * steps_j + 1.0) / (2.0 * degree))

def lagrange_table(nodes_at, points):
    degree = nodes_at.shape[0]
    differ = points[None, :] - nodes_at[:, None]
    diagonal_mask = jnp.eye(degree, dtype=bool)
    factors = jnp.where(diagonal_mask[:, :, None], 1.0, differ[None, :, :])
    numerator = jnp.prod(factors, axis=1)
    node_gaps = nodes_at[:, None] - nodes_at[None, :] + jnp.eye(degree, dtype=nodes_at.dtype)
    return numerator / jnp.prod(node_gaps, axis=1)[:, None]

def child_table(degree):
    chebyshev = cheb_nodes(degree)
    halves = jnp.stack([lagrange_table(chebyshev, child_side - 0.5 + 0.5 * chebyshev) for child_side in (0.0, 1.0)])
    interp_table = jnp.einsum('uaj,vbk->abuvjk', halves, halves)
    return interp_table.reshape(degree * degree, 4 * degree * degree)

def proxy_offsets(degree, grid_cells):
    chebyshev = cheb_nodes(degree)
    source_side = grid_cells // 32
    quarter = source_side / 4.0
    child_half = jnp.arange(2, dtype=jnp.float32) * (source_side / 2.0)
    along = child_half[:, None] + (quarter - 0.5) + quarter * chebyshev[None, :]
    child_x = jnp.broadcast_to(along[:, None, :, None], (2, 2, degree, degree)).reshape(-1)
    child_y = jnp.broadcast_to(along[None, :, None, :], (2, 2, degree, degree)).reshape(-1)
    parent_along = source_side / 2.0 - 0.5 + source_side / 2.0 * chebyshev
    parent_x = jnp.broadcast_to(parent_along[:, None], (degree, degree)).reshape(-1)
    parent_y = jnp.broadcast_to(parent_along[None, :], (degree, degree)).reshape(-1)
    return (child_x, child_y, parent_x, parent_y)

def phase_cycles(head_x, head_y, denominator, corner_x, corner_y, shift_x, shift_y):
    whole_part = jnp.mod(head_x * corner_x + head_y * corner_y, denominator).astype(jnp.float32) / denominator
    place_x = head_x.astype(jnp.float32) / denominator
    place_y = head_y.astype(jnp.float32) / denominator
    turn_x = TWO_PI * jnp.mod(speed_waves * head_x, denominator).astype(jnp.float32) / denominator
    turn_y = TWO_PI * jnp.mod(speed_waves * head_y, denominator).astype(jnp.float32) / denominator
    speed_x = (2.0 + jnp.sin(turn_x) * jnp.sin(turn_y)) / 16.0
    speed_y = (2.0 + jnp.cos(turn_x) * jnp.cos(turn_y)) / 16.0
    freq_x = corner_x.astype(jnp.float32) + shift_x
    freq_y = corner_y.astype(jnp.float32) + shift_y
    return whole_part + place_x * shift_x + place_y * shift_y + jnp.sqrt((speed_x * freq_x) ** 2 + (speed_y * freq_y) ** 2)

def target_centres(box_ids, grid_cells):
    target_side = grid_cells // 64
    target_row = grid_cells // 32
    return (2 * (box_ids // target_row) * target_side + target_side - 1, 2 * (box_ids % target_row) * target_side + target_side - 1)

def pivot_points(box_ids, pivot_ids, grid_cells):
    target_side = grid_cells // 64
    target_row = grid_cells // 32
    return (box_ids // target_row * target_side + pivot_ids // target_side, box_ids % target_row * target_side + pivot_ids % target_side)

def source_box(child_box, box_id, centre_x, centre_y, offsets, interp_table, grid_cells):
    child_x, child_y, parent_x, parent_y = offsets
    corner_x = box_id // (grid_cells // 64) * (grid_cells // 32) - grid_cells // 2
    corner_y = box_id % (grid_cells // 64) * (grid_cells // 32) - grid_cells // 2
    half_row = grid_cells // 64
    inner = child_box.shape[1]
    parents = child_box.shape[2]
    spread = child_box.reshape(2, inner, parents // half_row, 1, half_row, 1)
    spread = jnp.broadcast_to(spread, (2, inner, parents // half_row, 2, half_row, 2)).reshape(2, inner, 4 * parents)
    phase_now = TWO_PI * phase_cycles(centre_x[None, :], centre_y[None, :], 2 * grid_cells, corner_x, corner_y, child_x[:, None], child_y[:, None])
    cosine = jnp.cos(phase_now)
    sine_part = jnp.sin(phase_now)
    stacked = jnp.stack([spread[0] * cosine + spread[1] * sine_part, spread[1] * cosine - spread[0] * sine_part])
    interp = jnp.einsum('tc,zca->zta', interp_table, stacked, precision=lax.Precision.HIGHEST)
    phase_back = TWO_PI * phase_cycles(centre_x[None, :], centre_y[None, :], 2 * grid_cells, corner_x, corner_y, parent_x[:, None], parent_y[:, None])
    cosine_back = jnp.cos(phase_back)
    sine_back = jnp.sin(phase_back)
    return jnp.stack([interp[0] * cosine_back - interp[1] * sine_back, interp[0] * sine_back + interp[1] * cosine_back])

def skeleton_rows(point_x, point_y, box_ids, weights, offsets, grid_cells):
    parent_x = offsets[2]
    parent_y = offsets[3]
    corner_x = box_ids // (grid_cells // 64) * (grid_cells // 32) - grid_cells // 2
    corner_y = box_ids % (grid_cells // 64) * (grid_cells // 32) - grid_cells // 2
    phase_now = TWO_PI * phase_cycles(point_x[None, None, :], point_y[None, None, :], grid_cells, corner_x[:, None, None], corner_y[:, None, None], parent_x[None, :, None], parent_y[None, :, None])
    cosine = jnp.cos(phase_now)
    sine_part = jnp.sin(phase_now)
    real_sum = lax.optimization_barrier(jnp.sum(cosine * weights[:, 0] - sine_part * weights[:, 1], axis=1))
    imag_sum = lax.optimization_barrier(jnp.sum(sine_part * weights[:, 0] + cosine * weights[:, 1], axis=1))
    return jnp.stack([real_sum, imag_sum])

def reference(child_weights, pivots, ranks, owner_slot):
    grid_cells = GRID
    interp_table = child_table(Q)
    offsets = proxy_offsets(Q, grid_cells)
    targets_all = jnp.arange(NA, dtype=jnp.int32)
    centre_x, centre_y = target_centres(targets_all, grid_cells)

    def one_box(box_id):
        child_box = lax.dynamic_index_in_dim(child_weights, box_id, 1, keepdims=False).reshape(2, 4 * Q * Q, NA // 4)
        return source_box(child_box, box_id, centre_x, centre_y, offsets, interp_table, grid_cells)
    weights = lax.map(one_box, jnp.arange(NSB, dtype=jnp.int32))
    live_total = NA * RMEAN
    rank_ends = jnp.cumsum(ranks).astype(jnp.int32)
    starts = rank_ends - ranks
    live_rows = jnp.arange(live_total, dtype=jnp.int32)
    live_box = jnp.searchsorted(rank_ends, live_rows, side='right').astype(jnp.int32)
    live_rank = live_rows - starts[live_box]
    live_pivot = pivots[live_box, live_rank]
    point_x, point_y = pivot_points(live_box, live_pivot, grid_cells)
    block_rows = math.gcd(live_total, 256)
    box_ids = jnp.arange(NSB, dtype=jnp.int32)

    def one_block(block_args):
        box_block, x_block, y_block = block_args
        gathered = jnp.take(weights, box_block, axis=3)
        return skeleton_rows(x_block, y_block, box_ids, gathered, offsets, grid_cells)
    block_parts = lax.map(one_block, (live_box.reshape(-1, block_rows), point_x.reshape(-1, block_rows), point_y.reshape(-1, block_rows)))
    live_values = jnp.moveaxis(block_parts, 0, 2).reshape(2, NSB, live_total)
    slot_box = jnp.argsort(owner_slot).astype(jnp.int32)
    rank_ids = jnp.arange(RT, dtype=jnp.int32)
    padded_index = jnp.minimum(starts[slot_box][None, :] + rank_ids[:, None], live_total - 1)
    valid_rows = rank_ids[:, None] < ranks[slot_box][None, :]
    padded = jnp.where(valid_rows[None, None], live_values[:, :, padded_index], 0.0)
    grouped = padded.reshape(2, NSB // 64, 2, grid_cells // 128, 2, RT, NA).sum(axis=(2, 4))
    grouped = grouped.reshape(2, NP, RT, NA)
    return jnp.transpose(grouped, (0, 2, 3, 1))
```

```python
import numpy as np

import jax
import jax.numpy as jnp
from jax import lax
from jax.experimental import pallas as pl
from jax.experimental.pallas import tpu as pltpu
from jax.sharding import PartitionSpec as P

AXES = ("grp", "dev")
F32 = jnp.float32
BF16 = jnp.bfloat16
I32 = jnp.int32

SIN_C = (2.6417391300201416, -1.0859273672103882, 0.13053695857524872)
SIN_FINE = (2.641753911972046, -1.0863757133483887, 0.1339970976114273, -0.007720405701547861)
ROOT2 = 1.4142135623730951
ROOT8 = 2.8284271247461903


def _f32(x):
    return np.float32(x)


CHEB = [_f32(np.cos(np.pi * (2 * j + 1) / 16.0)) for j in range(8)]
PARENT_OFF = [float(_f32(31.5) + _f32(32.0) * c) for c in CHEB]
CHILD_OFF = [[float(_f32(32.0 * u + 15.5) + _f32(16.0) * c) for c in CHEB] for u in range(2)]


def interp_matrix():
    nodes = np.cos(np.pi * (2 * np.arange(8) + 1) / 16.0)
    halves = np.zeros((2, 8, 8))
    for u in range(2):
        points = u - 0.5 + 0.5 * nodes
        for t in range(8):
            value = np.ones(8)
            for s in range(8):
                if s != t:
                    value = value * (points - nodes[s]) / (nodes[t] - nodes[s])
            halves[u, t] = value
    full = np.einsum("uaj,vbk->abuvjk", halves, halves).reshape(64, 256)
    return full.astype(np.float32)


def class_turns(off_x, off_y, sign):
    lane = np.arange(256)
    a, b = lane // 128, (lane % 32) // 4
    cycles = (np.outer(off_x, a) + np.outer(off_y, b)) / 8.0
    angle = sign * 2.0 * np.pi * (cycles % 1.0)
    return np.stack([np.cos(angle), np.sin(angle)]).astype(np.float32)


def wrap(x):
    return x - jnp.round(x)


def sine_parts(phase, coef):
    r = wrap(phase)
    z = r * r
    s = coef[-1]
    for c in coef[-2::-1]:
        s = s * z + c
    s = s * r
    q = s * s
    w = ROOT8 - q
    v = 1.0 / lax.rsqrt(w)
    return q * w, (s * v) * (ROOT2 - q)


def cos_sin(phase, coef=SIN_C):
    d, s = sine_parts(phase, coef)
    return 1.0 - d, s


def root(x):
    return 1.0 / lax.rsqrt(x)


def speeds(turn_x, turn_y):
    sub = lax.broadcasted_iota(I32, turn_x.shape, 0)
    c, s = cos_sin(jnp.where(sub < 4, turn_x, turn_y), SIN_FINE)
    c1 = (2.0 + s * pltpu.roll(s, 4, 0)) * 0.0625
    c2 = (2.0 + c * pltpu.roll(c, 4, 0)) * 0.0625
    return c1 * c1, c2 * c2


def split(x):
    hi = x.astype(BF16)
    return hi, (x - hi.astype(F32)).astype(BF16)


def by_sublane(values, like):
    sub = lax.broadcasted_iota(I32, like.shape, 0)
    out = jnp.full(like.shape, values[0], F32)
    for s in range(1, 8):
        out = jnp.where(sub == s, values[s], out)
    return out


def lanes_of(x, idx):
    return jnp.take_along_axis(x, idx, axis=1)


NT = (((1,), (1,)), ((), ()))


def source_kernel(
    pos_ref, w_ref, os_ref, ranks_ref, tab_ref, turn_c, turn_p, out_ref, excl_ref, rank_ref,
    perm, w_turned, mod_hi, mod_lo, d_hi, d_lo, wave,
):
    step = pl.program_id(0)
    pos = pos_ref[0]
    lane = lax.broadcasted_iota(I32, (8, 128), 1)
    sub = lax.broadcasted_iota(I32, (8, 128), 0)

    @pl.when(step == 0)
    def _():
        ranks = ranks_ref[...].astype(F32)
        owners = os_ref[...].astype(F32)
        rank_row = []
        for n in range(8):
            e1, e2, half = n // 4, (n // 2) % 2, n % 2
            idx = e1 * 64 + 2 * (lane % 32) + e2
            mine = sub == 4 * half + lane // 32
            at = jnp.sum(jnp.where(mine, lanes_of(owners, idx), 0.0), axis=0, keepdims=True)
            rk = jnp.sum(jnp.where(mine, lanes_of(ranks, idx), 0.0), axis=0, keepdims=True)
            rank_row.append(jnp.broadcast_to(rk, (8, 128)))
            at = jnp.broadcast_to(at, (128, 128)).astype(I32)
            slot = lax.broadcasted_iota(I32, (128, 128), 0)
            for j in range(8):
                hit = jnp.where(slot + j * 128 == at, 1.0, 0.0)
                perm[j * 128 : j * 128 + 128, n * 128 : n * 128 + 128] = hit.astype(BF16)
        rank_rows = jnp.concatenate(rank_row, axis=1).astype(BF16)
        upto = (
            lax.broadcasted_iota(I32, (128, 128), 0) <= lax.broadcasted_iota(I32, (128, 128), 1)
        )
        upto = jnp.where(upto, 1.0, 0.0).astype(BF16)
        for j in range(8):
            rk = lax.dot_general(
                rank_rows, perm[j * 128 : j * 128 + 128, :], NT, preferred_element_type=F32
            )
            run = jnp.dot(rk.astype(BF16), upto, preferred_element_type=F32)
            rank_ref[j : j + 1, :] = rk[0:1].astype(I32)
            excl_ref[j : j + 1, :] = (run - rk)[0:1].astype(I32)

    def move(at):
        moved = lax.dot_general(d_hi[...], perm[...], NT, preferred_element_type=F32)
        moved = moved + lax.dot_general(d_lo[...], perm[...], NT, preferred_element_type=F32)
        for j in range(8):
            out_ref[j, pl.ds(at, 128, stride=8), :] = moved[:, j * 128 : j * 128 + 128]

    move(jnp.maximum(step - 1, 0))

    box = 2 * (step % 4) + step // 4
    corner_xf = (64 * (pos // 4) - 1024).astype(F32)
    corner_yf = (64 * ((pos % 4) * 8 + box) - 1024).astype(F32)
    h_x = 64 * ((lane % 64) // 8) + 31
    h_y = 64 * (lane % 8) + 31
    h_xf, h_yf = h_x.astype(F32), h_y.astype(F32)
    sq_x, sq_y = speeds(h_xf * (1.0 / 512), h_yf * (1.0 / 512))
    x, y = h_xf * (1.0 / 4096), h_yf * (1.0 / 4096)
    high = lane >= 64

    off_y = jnp.where(high, by_sublane(CHILD_OFF[1], lane), by_sublane(CHILD_OFF[0], lane))
    k_y = corner_yf + off_y
    part_y, line_y = sq_y * (k_y * k_y), y * off_y
    for u in range(2):
        for j1 in range(8):
            off_x = CHILD_OFF[u][j1]
            k_x = corner_xf + off_x
            c, s = cos_sin(root(sq_x * (k_x * k_x) + part_y) + (x * off_x + line_y))
            wave[0, (u * 8 + j1) * 8 : (u * 8 + j1) * 8 + 8, :] = c
            wave[1, (u * 8 + j1) * 8 : (u * 8 + j1) * 8 + 8, :] = s
    off_y = by_sublane(PARENT_OFF, lane)
    k_y = corner_yf + off_y
    part_y, line_y = sq_y * (k_y * k_y), y * off_y
    for m in range(4):
        off_x = jnp.where(high, PARENT_OFF[2 * m + 1], PARENT_OFF[2 * m])
        k_x = corner_xf + off_x
        c, s = cos_sin(root(sq_x * (k_x * k_x) + part_y) + (x * off_x + line_y))
        wave[0, 128 + m * 8 : 136 + m * 8, :] = c
        wave[1, 128 + m * 8 : 136 + m * 8, :] = s

    for part in range(4):
        rows = slice(part * 64, part * 64 + 64)
        w_re, w_im = w_ref[0, 0, rows, :], w_ref[1, 0, rows, :]
        t_re, t_im = turn_c[0, rows, :], turn_c[1, rows, :]
        w_turned[0, rows, :] = w_re * t_re - w_im * t_im
        w_turned[1, rows, :] = w_re * t_im + w_im * t_re

    for e in range(4):
        e1, e2 = e // 2, e % 2
        pick = (2 * (lane // 32) + e1) * 8 + 2 * (lane % 4) + e2
        for u in range(2):
            for v in range(2):
                idx = pick + v * 64
                for g in range(4):
                    base = (u * 8 + 2 * g) * 8
                    c = jnp.concatenate(
                        [lanes_of(wave[0, base + 8 * i : base + 8 * i + 8, :], idx) for i in (0, 1)]
                    )
                    s = jnp.concatenate(
                        [lanes_of(wave[1, base + 8 * i : base + 8 * i + 8, :], idx) for i in (0, 1)]
                    )
                    at = (u * 2 + v) * 64 + g * 16
                    rows = slice(at, at + 16)
                    for half in range(2):
                        w_re = w_turned[0, rows, half * 128 : half * 128 + 128]
                        w_im = w_turned[1, rows, half * 128 : half * 128 + 128]
                        col = e * 512 + half * 128
                        hi, lo = split(w_re * c + w_im * s)
                        mod_hi[rows, col : col + 128] = hi
                        mod_lo[rows, col : col + 128] = lo
                        hi, lo = split(w_im * c - w_re * s)
                        mod_hi[rows, col + 256 : col + 384] = hi
                        mod_lo[rows, col + 256 : col + 384] = lo
        cols = slice(e * 512, e * 512 + 512)
        first = jnp.dot(tab_ref[...], mod_hi[:, cols], preferred_element_type=F32)
        second = jnp.dot(tab_ref[0:64, :], mod_lo[:, cols], preferred_element_type=F32)
        interp = first[0:64] + (first[64:128] + second)
        c = jnp.concatenate(
            [
                lanes_of(wave[0, 128 + (t // 2) * 8 : 136 + (t // 2) * 8, :], pick + (t % 2) * 64)
                for t in range(8)
            ]
        )
        s = jnp.concatenate(
            [
                lanes_of(wave[1, 128 + (t // 2) * 8 : 136 + (t // 2) * 8, :], pick + (t % 2) * 64)
                for t in range(8)
            ]
        )
        for half in range(2):
            i_re = interp[:, half * 128 : half * 128 + 128]
            i_im = interp[:, half * 128 + 256 : half * 128 + 384]
            t_re = turn_p[0, :, half * 128 : half * 128 + 128]
            t_im = turn_p[1, :, half * 128 : half * 128 + 128]
            g_re = i_re * t_re - i_im * t_im
            g_im = i_re * t_im + i_im * t_re
            col = (e * 2 + half) * 128
            hi, lo = split(g_re * c - g_im * s)
            d_hi[0:64, col : col + 128] = hi
            d_lo[0:64, col : col + 128] = lo
            hi, lo = split(g_re * s + g_im * c)
            d_hi[64:128, col : col + 128] = hi
            d_lo[64:128, col : col + 128] = lo

    @pl.when(step == 7)
    def _():
        move(7)


def source_stage(pos, weights, owner_slot, ranks):
    table = interp_matrix()
    hi = table.astype(jnp.bfloat16)
    lo = (table - hi.astype(np.float32)).astype(jnp.bfloat16)
    stacked = jnp.asarray(np.concatenate([hi, lo], axis=0))
    child = np.array(CHILD_OFF)
    row = np.arange(256)
    off_x = child[row // 128, (row // 8) % 8]
    off_y = child[(row // 64) % 2, row % 8]
    parent = np.array(PARENT_OFF)
    turn_c = jnp.asarray(class_turns(off_x, off_y, -1.0))
    turn_p = jnp.asarray(class_turns(parent[row[:64] // 8], parent[row[:64] % 8], 1.0))

    def whole(*shape):
        return pl.BlockSpec(shape, lambda g, p: (0,) * len(shape))

    return pl.pallas_call(
        source_kernel,
        out_shape=[
            jax.ShapeDtypeStruct((8, 1024, 128), F32),
            jax.ShapeDtypeStruct((8, 128), I32),
            jax.ShapeDtypeStruct((8, 128), I32),
        ],
        grid_spec=pltpu.PrefetchScalarGridSpec(
            num_scalar_prefetch=1,
            grid=(8,),
            in_specs=[
                pl.BlockSpec((2, 1, 256, 256), lambda g, p: (0, 2 * (g % 4) + g // 4, 0, 0)),
                whole(8, 128),
                whole(8, 128),
                whole(128, 256),
                whole(2, 256, 256),
                whole(2, 64, 256),
            ],
            out_specs=[whole(8, 1024, 128), whole(8, 128), whole(8, 128)],
            scratch_shapes=[
                pltpu.VMEM((1024, 1024), BF16),
                pltpu.VMEM((2, 256, 256), F32),
                pltpu.VMEM((256, 2048), BF16),
                pltpu.VMEM((256, 2048), BF16),
                pltpu.VMEM((128, 1024), BF16),
                pltpu.VMEM((128, 1024), BF16),
                pltpu.VMEM((2, 160, 128), F32),
            ],
        ),
        name="source_stage",
    )(pos, weights, owner_slot, ranks, stacked, turn_c, turn_p)


def target_kernel(
    pos_ref, excl_ref, rank_ref, delta_ref, piv_ref, os_ref, excl_v, rank_v, out_ref,
    digits, points_x, points_y, sums, rows_x, tiles, base,
):
    pos = pos_ref[0]
    lane = lax.broadcasted_iota(I32, (8, 128), 1)
    sub = lax.broadcasted_iota(I32, (8, 128), 0)
    sub32 = lax.broadcasted_iota(I32, (32, 128), 0).astype(F32)
    corner_x = 64 * (pos // 4) - 1024
    turn_x = corner_x.astype(F32) * (1.0 / 2048)
    corner_y = (64 * ((pos % 4) * 8 + 2 * (sub % 4) + sub // 4) - 1024).astype(F32)
    turn_y = corner_y * (1.0 / 2048)
    k_sq_y = []
    for off in PARENT_OFF:
        k_y = corner_y + off
        k_sq_y.append(k_y * k_y)
    off_col = by_sublane(PARENT_OFF, lane)
    k_x = corner_x.astype(F32) + off_col
    k_sq_x = k_x * k_x

    for n in range(8):
        p = piv_ref[n * 16 : n * 16 + 16].reshape(128, 128).astype(F32)
        p = jnp.transpose(p)[0:32, :].astype(I32)
        cols = slice(n * 128, n * 128 + 128)
        digits[0:32, cols] = (p // 32).astype(F32).astype(BF16)
        digits[32:64, cols] = (p % 32).astype(F32).astype(BF16)
        box = n * 128 + lax.broadcasted_iota(I32, (16, 128), 1)
        which = lax.broadcasted_iota(I32, (16, 128), 0)
        place = jnp.where(which == 0, box // 64, jnp.where(which == 1, box % 64, 0))
        digits[64:80, cols] = place.astype(F32).astype(BF16)

    def one_block(j, first_tile):
        slot = lax.broadcasted_iota(I32, (128, 128), 0) + j * 128
        got = jnp.zeros((80, 128), F32)
        for n in range(8):
            at = jnp.broadcast_to(os_ref[n : n + 1, :], (128, 128))
            hit = jnp.where(slot == at, 1.0, 0.0).astype(BF16)
            got = got + lax.dot_general(
                digits[:, n * 128 : n * 128 + 128], hit, NT, preferred_element_type=F32
            )
        points_x[...] = got[0:32] + 32.0 * got[64:65]
        points_y[...] = got[32:64] + 32.0 * got[65:66]
        start_row = jnp.broadcast_to(excl_v[pl.ds(j, 1), :], (8, 128)).astype(F32)
        end_row = start_row + jnp.broadcast_to(rank_v[pl.ds(j, 1), :], (8, 128)).astype(F32)
        ends_low = lanes_of(end_row, 8 * sub + 7)
        ends_high = lanes_of(end_row, 64 + 8 * sub + 7)
        ends_in = lanes_of(end_row, jnp.minimum(8 * lane + sub, 127))
        total_re = jnp.zeros((8, 128), F32)
        total_im = jnp.zeros((8, 128), F32)
        for t in range(64):
            total_re = total_re + delta_ref[j, t * 8 : t * 8 + 8, :]
            total_im = total_im + delta_ref[j, 512 + t * 8 : 520 + t * 8, :]
        sums[0:8, :] = total_re
        sums[8:16, :] = total_im
        base[j] = first_tile
        live = excl_ref[j, 127] + rank_ref[j, 127]
        n_tiles = (live + 127) // 128

        def one_tile(k, carry):
            row = (k * 128 + lane).astype(F32)
            ahead = jnp.where(ends_low <= row, 1.0, 0.0) + jnp.where(ends_high <= row, 1.0, 0.0)
            group = jnp.minimum(jnp.sum(ahead, axis=0, keepdims=True), 15.0)
            group = jnp.broadcast_to(group, (8, 128))
            inner = jnp.where(lanes_of(ends_in, group.astype(I32)) <= row, 1.0, 0.0)
            inner = jnp.broadcast_to(jnp.sum(inner, axis=0, keepdims=True), (8, 128))
            idx = jnp.minimum(8.0 * group + inner, 127.0).astype(I32)
            place = row - lanes_of(start_row, idx)
            idx32 = jnp.concatenate([idx] * 4)
            mine = sub32 == jnp.concatenate([place] * 4)
            got_x = jnp.where(mine, lanes_of(points_x[...], idx32), 0.0)
            got_y = jnp.where(mine, lanes_of(points_y[...], idx32), 0.0)
            h_x = jnp.broadcast_to(jnp.sum(got_x, axis=0, keepdims=True), (8, 128))
            h_y = jnp.broadcast_to(jnp.sum(got_y, axis=0, keepdims=True), (8, 128))
            sq_x, sq_y = speeds(h_x * (1.0 / 256), h_y * (1.0 / 256))
            x, y = h_x * (1.0 / 2048), h_y * (1.0 / 2048)
            rows_x[0:8, :] = sq_x * k_sq_x
            rows_x[8:16, :] = wrap(h_x * turn_x) + x * off_col
            part_y = [sq_y * k_sq for k_sq in k_sq_y]
            whole_y = wrap(h_y * turn_y)
            line_y = [wrap(whole_y + y * off) for off in PARENT_OFF]
            acc_re = lanes_of(sums[0:8, :], idx)
            acc_im = lanes_of(sums[8:16, :], idx)
            for t1 in range(8):
                part_x = jnp.broadcast_to(rows_x[t1 : t1 + 1, :], (8, 128))
                line_x = jnp.broadcast_to(rows_x[8 + t1 : 9 + t1, :], (8, 128))
                for t2 in range(8):
                    t = t1 * 8 + t2
                    d_re = lanes_of(delta_ref[j, t * 8 : t * 8 + 8, :], idx)
                    d_im = lanes_of(delta_ref[j, 512 + t * 8 : 520 + t * 8, :], idx)
                    d, s = sine_parts(root(part_x + part_y[t2]) + (line_x + line_y[t2]), SIN_C)
                    acc_re = acc_re - (d * d_re + s * d_im)
                    acc_im = acc_im + (s * d_re - d * d_im)
            acc_re = acc_re + pltpu.roll(acc_re, 4, 0)
            acc_im = acc_im + pltpu.roll(acc_im, 4, 0)
            tiles[carry] = jnp.where(sub < 4, acc_re, acc_im)
            return carry + 1

        return lax.fori_loop(0, n_tiles, one_tile, first_tile)

    lax.fori_loop(0, 8, one_block, 0)

    def one_owner(o, _):
        place = base[o // 16] * 128 + excl_ref[o // 16, (o % 16) * 8]
        tile = place // 128
        shift = (128 - place % 128) % 128
        keep = lane < 128 - place % 128
        a = pltpu.roll(tiles[tile], shift, 1)
        b = pltpu.roll(tiles[tile + 1], shift, 1)
        c = pltpu.roll(tiles[tile + 2], shift, 1)
        out_ref[o, :, 0:128] = jnp.where(keep, a, b)
        out_ref[o, :, 128:256] = jnp.where(keep, b, c)
        return 0

    lax.fori_loop(0, 128, one_owner, 0, unroll=8)


def target_stage(pos, excl, rank, delta, piv, owner_slot):
    smem = pl.BlockSpec(memory_space=pltpu.SMEM)
    vmem = pl.BlockSpec(memory_space=pltpu.VMEM)
    return pl.pallas_call(
        target_kernel,
        out_shape=jax.ShapeDtypeStruct((128, 8, 256), F32),
        in_specs=[smem, smem, smem, vmem, vmem, vmem, vmem, vmem],
        out_specs=vmem,
        scratch_shapes=[
            pltpu.VMEM((80, 1024), BF16),
            pltpu.VMEM((32, 128), F32),
            pltpu.VMEM((32, 128), F32),
            pltpu.VMEM((16, 128), F32),
            pltpu.VMEM((16, 128), F32),
            pltpu.VMEM((96, 8, 128), F32),
            pltpu.SMEM((8,), I32),
        ],
        name="target_stage",
    )(pos, excl, rank, delta, piv, owner_slot, excl, rank)


def owner_kernel(pos_ref, excl_ref, rank_ref, in_ref, out_ref, gathered, rows):
    pos = pos_ref[0]
    at = (pos % 16) * 8
    sub = lax.broadcasted_iota(I32, (8, 256), 0)
    for p1 in range(16):
        part = [in_ref[p1 * 8 + q] + in_ref[p1 * 8 + 4 + q] for q in range(4)]
        for m in range(2):
            even, odd = part[2 * m], part[2 * m + 1]
            row = p1 * 16 + m * 8
            gathered[0, row : row + 8, :] = jnp.where(sub < 4, even, pltpu.roll(odd, 4, 0))
            gathered[1, row : row + 8, :] = jnp.where(sub < 4, pltpu.roll(even, 4, 0), odd)
    for z in range(2):
        turned = jnp.transpose(gathered[z])
        for half in range(2):
            rows[pl.ds(z * 2 + half, 256, stride=8), :] = turned[:, half * 128 : half * 128 + 128]
    i = lax.broadcasted_iota(I32, (32, 128), 0)
    for k in range(8):
        start = excl_ref[pos // 16, at + k] - excl_ref[pos // 16, at]
        live = i < rank_ref[pos // 16, at + k]
        for z in range(2):
            for half in range(2):
                got = rows[pl.ds(start * 8 + (z * 2 + half), 32, stride=8), :]
                out_ref[z, :, k, half * 128 : half * 128 + 128] = jnp.where(live, got, 0.0)


def owner_stage(pos, excl, rank, received):
    smem = pl.BlockSpec(memory_space=pltpu.SMEM)
    vmem = pl.BlockSpec(memory_space=pltpu.VMEM)
    return pl.pallas_call(
        owner_kernel,
        out_shape=jax.ShapeDtypeStruct((2, 32, 8, 256), F32),
        in_specs=[smem, smem, smem, vmem],
        out_specs=vmem,
        scratch_shapes=[pltpu.VMEM((2, 256, 256), F32), pltpu.VMEM((2048, 128), F32)],
        name="owner_stage",
    )(pos, excl, rank, received)


def local(child_weights, pivots, ranks, owner_slot):
    pos = lax.axis_index("grp") * lax.axis_size("dev") + lax.axis_index("dev")
    pos = pos.astype(I32).reshape(1)
    spread = jnp.broadcast_to(jnp.pad(pivots, ((0, 0), (0, 96)))[None], (128, 8, 128))
    all_pivots = lax.all_to_all(spread, AXES, split_axis=0, concat_axis=0, tiled=True)
    at = owner_slot.reshape(8, 128)
    weights = child_weights.reshape(2, 8, 256, 256)
    delta, excl, rank = source_stage(pos, weights, at, ranks.reshape(8, 128))
    send = target_stage(pos, excl, rank, delta, all_pivots, at)
    received = lax.all_to_all(send, AXES, split_axis=0, concat_axis=0, tiled=True)
    return owner_stage(pos, excl, rank, received)


def solution(mesh):
    in_specs = (P(None, AXES, None, None, None), P(AXES, None), P(), P())
    out_specs = P(None, None, AXES, None)
    return jax.shard_map(local, mesh=mesh, in_specs=in_specs, out_specs=out_specs, check_vma=False)
```

```python
import numpy as np

import jax
import jax.numpy as jnp
from jax import lax
from jax.experimental import pallas as pl
from jax.experimental.pallas import tpu as pltpu
from jax.sharding import PartitionSpec as P

AXES = ("grp", "dev")
F32 = jnp.float32
BF16 = jnp.bfloat16
I32 = jnp.int32

SIN_C = (2.6417391300201416, -1.0859273672103882, 0.13053695857524872)
SIN_FINE = (2.641753911972046, -1.0863757133483887, 0.1339970976114273, -0.007720405701547861)
ROOT2 = 1.4142135623730951
ROOT8 = 2.8284271247461903


def _f32(x):
    return np.float32(x)


CHEB = [_f32(np.cos(np.pi * (2 * j + 1) / 16.0)) for j in range(8)]
PARENT_OFF = [float(_f32(31.5) + _f32(32.0) * c) for c in CHEB]
CHILD_OFF = [[float(_f32(32.0 * u + 15.5) + _f32(16.0) * c) for c in CHEB] for u in range(2)]


def interp_matrix():
    nodes = np.cos(np.pi * (2 * np.arange(8) + 1) / 16.0)
    halves = np.zeros((2, 8, 8))
    for u in range(2):
        points = u - 0.5 + 0.5 * nodes
        for t in range(8):
            value = np.ones(8)
            for s in range(8):
                if s != t:
                    value = value * (points - nodes[s]) / (nodes[t] - nodes[s])
            halves[u, t] = value
    full = np.einsum("uaj,vbk->abuvjk", halves, halves).reshape(64, 256)
    return full.astype(np.float32)


def class_turns(off_x, off_y, sign):
    lane = np.arange(256)
    a, b = lane // 128, (lane % 32) // 4
    cycles = (np.outer(off_x, a) + np.outer(off_y, b)) / 8.0
    angle = sign * 2.0 * np.pi * (cycles % 1.0)
    return np.stack([np.cos(angle), np.sin(angle)]).astype(np.float32)


def wrap(x):
    return x - jnp.round(x)


def sine_parts(phase, coef):
    r = wrap(phase)
    z = r * r
    s = coef[-1]
    for c in coef[-2::-1]:
        s = s * z + c
    s = s * r
    q = s * s
    w = ROOT8 - q
    v = w * lax.rsqrt(w)
    return q * w, (s * v) * (ROOT2 - q)


def cos_sin(phase, coef=SIN_C):
    d, s = sine_parts(phase, coef)
    return 1.0 - d, s


def root(x):
    return x * lax.rsqrt(x)


def speeds(turn_x, turn_y):
    sub = lax.broadcasted_iota(I32, turn_x.shape, 0)
    c, s = cos_sin(jnp.where(sub < 4, turn_x, turn_y), SIN_FINE)
    c1 = (2.0 + s * pltpu.roll(s, 4, 0)) * 0.0625
    c2 = (2.0 + c * pltpu.roll(c, 4, 0)) * 0.0625
    return c1 * c1, c2 * c2


def split(x):
    hi = x.astype(BF16)
    return hi, (x - hi.astype(F32)).astype(BF16)


def by_sublane(values, like):
    sub = lax.broadcasted_iota(I32, like.shape, 0)
    out = jnp.full(like.shape, values[0], F32)
    for s in range(1, 8):
        out = jnp.where(sub == s, values[s], out)
    return out


def lanes_of(x, idx):
    return jnp.take_along_axis(x, idx, axis=1)


NT = (((1,), (1,)), ((), ()))


def source_kernel(
    pos_ref, w_ref, os_ref, ranks_ref, tab_ref, turn_c, turn_p,
    out_ref, excl_ref, rank_ref, slot_at_ref, slot_rank_ref,
    w_turned, mod_hi, mod_lo, wave, labels,
):
    step = pl.program_id(0)
    pos = pos_ref[0]
    lane = lax.broadcasted_iota(I32, (8, 128), 1)
    sub = lax.broadcasted_iota(I32, (8, 128), 0)

    @pl.when(step == 0)
    def _():
        ranks = ranks_ref[...].astype(F32)
        owners = os_ref[...].astype(F32)
        rank8 = jnp.zeros((8, 128), F32)
        at_row = []
        for n in range(8):
            e1, e2, half = n // 4, (n // 2) % 2, n % 2
            idx = e1 * 64 + 2 * (lane % 32) + e2
            mine = sub == 4 * half + lane // 32
            at_row.append(
                jnp.sum(jnp.where(mine, lanes_of(owners, idx), 0.0), axis=0, keepdims=True)
            )
            rk = jnp.sum(jnp.where(mine, lanes_of(ranks, idx), 0.0), axis=0, keepdims=True)
            rank8 = jnp.where(sub == n, jnp.broadcast_to(rk, (8, 128)), rank8)
        upto = (
            lax.broadcasted_iota(I32, (128, 128), 0) <= lax.broadcasted_iota(I32, (128, 128), 1)
        )
        upto = jnp.where(upto, 1.0, 0.0).astype(BF16)
        excl8 = jnp.dot(rank8.astype(BF16), upto, preferred_element_type=F32) - rank8
        rank_ref[...] = rank8.astype(I32)
        excl_ref[...] = excl8.astype(I32)
        row = lax.broadcasted_iota(I32, (16, 128), 0)
        for n in range(8):
            rk = jnp.broadcast_to(rank8[n : n + 1], (16, 128))
            ahead = jnp.broadcast_to(excl8[n : n + 1], (16, 128)).astype(I32)
            high, low = (ahead >> 6).astype(F32), (ahead & 63).astype(F32)
            label = jnp.where(row == 2, high, jnp.where(row == 3, low, 0.0))
            label = jnp.where(row == 0, rk, jnp.where(row == 1, float(n), label))
            labels[:, n * 128 : n * 128 + 128] = label.astype(BF16)
        for j in range(8):
            slot = lax.broadcasted_iota(I32, (128, 128), 0).astype(F32) + j * 128.0
            got = jnp.zeros((16, 128), F32)
            for n in range(8):
                hit = jnp.where(slot == jnp.broadcast_to(at_row[n], (128, 128)), 1.0, 0.0)
                got = got + lax.dot_general(
                    labels[:, n * 128 : n * 128 + 128], hit.astype(BF16), NT,
                    preferred_element_type=F32,
                )
            slot_rank_ref[j : j + 1, :] = got[0:1].astype(I32)
            at = got[1:2] * 8192.0 + got[2:3] * 64.0 + got[3:4]
            slot_at_ref[j : j + 1, :] = at.astype(I32)

    box = 2 * (step % 4) + step // 4
    corner_xf = (64 * (pos // 4) - 1024).astype(F32)
    corner_yf = (64 * ((pos % 4) * 8 + box) - 1024).astype(F32)
    h_x = 64 * ((lane % 64) // 8) + 31
    h_y = 64 * (lane % 8) + 31
    h_xf, h_yf = h_x.astype(F32), h_y.astype(F32)
    sq_x, sq_y = speeds(h_xf * (1.0 / 512), h_yf * (1.0 / 512))
    x, y = h_xf * (1.0 / 4096), h_yf * (1.0 / 4096)
    high = lane >= 64

    off_y = jnp.where(high, by_sublane(CHILD_OFF[1], lane), by_sublane(CHILD_OFF[0], lane))
    k_y = corner_yf + off_y
    part_y, line_y = sq_y * (k_y * k_y), y * off_y
    for u in range(2):
        for j1 in range(8):
            off_x = CHILD_OFF[u][j1]
            k_x = corner_xf + off_x
            c, s = cos_sin(root(sq_x * (k_x * k_x) + part_y) + (x * off_x + line_y))
            wave[0, (u * 8 + j1) * 8 : (u * 8 + j1) * 8 + 8, :] = c
            wave[1, (u * 8 + j1) * 8 : (u * 8 + j1) * 8 + 8, :] = s
    off_y = by_sublane(PARENT_OFF, lane)
    k_y = corner_yf + off_y
    part_y, line_y = sq_y * (k_y * k_y), y * off_y
    for m in range(4):
        off_x = jnp.where(high, PARENT_OFF[2 * m + 1], PARENT_OFF[2 * m])
        k_x = corner_xf + off_x
        c, s = cos_sin(root(sq_x * (k_x * k_x) + part_y) + (x * off_x + line_y))
        wave[0, 128 + m * 8 : 136 + m * 8, :] = c
        wave[1, 128 + m * 8 : 136 + m * 8, :] = s

    for part in range(4):
        rows = slice(part * 64, part * 64 + 64)
        w_re, w_im = w_ref[0, 0, rows, :], w_ref[1, 0, rows, :]
        t_re, t_im = turn_c[0, rows, :], turn_c[1, rows, :]
        w_turned[0, rows, :] = w_re * t_re - w_im * t_im
        w_turned[1, rows, :] = w_re * t_im + w_im * t_re

    for e in range(4):
        e1, e2 = e // 2, e % 2
        pick = (2 * (lane // 32) + e1) * 8 + 2 * (lane % 4) + e2
        for u in range(2):
            for v in range(2):
                idx = pick + v * 64
                for g in range(4):
                    base = (u * 8 + 2 * g) * 8
                    c = jnp.concatenate(
                        [lanes_of(wave[0, base + 8 * i : base + 8 * i + 8, :], idx) for i in (0, 1)]
                    )
                    s = jnp.concatenate(
                        [lanes_of(wave[1, base + 8 * i : base + 8 * i + 8, :], idx) for i in (0, 1)]
                    )
                    at = (u * 2 + v) * 64 + g * 16
                    rows = slice(at, at + 16)
                    for half in range(2):
                        w_re = w_turned[0, rows, half * 128 : half * 128 + 128]
                        w_im = w_turned[1, rows, half * 128 : half * 128 + 128]
                        col = e * 512 + half * 128
                        hi, lo = split(w_re * c + w_im * s)
                        mod_hi[rows, col : col + 128] = hi
                        mod_lo[rows, col : col + 128] = lo
                        hi, lo = split(w_im * c - w_re * s)
                        mod_hi[rows, col + 256 : col + 384] = hi
                        mod_lo[rows, col + 256 : col + 384] = lo
        cols = slice(e * 512, e * 512 + 512)
        first = jnp.dot(tab_ref[...], mod_hi[:, cols], preferred_element_type=F32)
        second = jnp.dot(tab_ref[0:64, :], mod_lo[:, cols], preferred_element_type=F32)
        interp = first[0:64] + (first[64:128] + second)
        c = jnp.concatenate(
            [
                lanes_of(wave[0, 128 + (t // 2) * 8 : 136 + (t // 2) * 8, :], pick + (t % 2) * 64)
                for t in range(8)
            ]
        )
        s = jnp.concatenate(
            [
                lanes_of(wave[1, 128 + (t // 2) * 8 : 136 + (t // 2) * 8, :], pick + (t % 2) * 64)
                for t in range(8)
            ]
        )
        for half in range(2):
            i_re = interp[:, half * 128 : half * 128 + 128]
            i_im = interp[:, half * 128 + 256 : half * 128 + 384]
            t_re = turn_p[0, :, half * 128 : half * 128 + 128]
            t_im = turn_p[1, :, half * 128 : half * 128 + 128]
            g_re = i_re * t_re - i_im * t_im
            g_im = i_re * t_im + i_im * t_re
            out_ref[e * 2 + half, pl.ds(step, 64, stride=8), :] = g_re * c - g_im * s
            out_ref[e * 2 + half, pl.ds(512 + step, 64, stride=8), :] = g_re * s + g_im * c


def source_stage(pos, weights, owner_slot, ranks):
    table = interp_matrix()
    hi = table.astype(jnp.bfloat16)
    lo = (table - hi.astype(np.float32)).astype(jnp.bfloat16)
    stacked = jnp.asarray(np.concatenate([hi, lo], axis=0))
    child = np.array(CHILD_OFF)
    row = np.arange(256)
    off_x = child[row // 128, (row // 8) % 8]
    off_y = child[(row // 64) % 2, row % 8]
    parent = np.array(PARENT_OFF)
    turn_c = jnp.asarray(class_turns(off_x, off_y, -1.0))
    turn_p = jnp.asarray(class_turns(parent[row[:64] // 8], parent[row[:64] % 8], 1.0))

    def whole(*shape):
        return pl.BlockSpec(shape, lambda g, p: (0,) * len(shape))

    return pl.pallas_call(
        source_kernel,
        out_shape=[
            jax.ShapeDtypeStruct((8, 1024, 128), F32),
            *[jax.ShapeDtypeStruct((8, 128), I32)] * 4,
        ],
        grid_spec=pltpu.PrefetchScalarGridSpec(
            num_scalar_prefetch=1,
            grid=(8,),
            in_specs=[
                pl.BlockSpec((2, 1, 256, 256), lambda g, p: (0, 2 * (g % 4) + g // 4, 0, 0)),
                whole(8, 128),
                whole(8, 128),
                whole(128, 256),
                whole(2, 256, 256),
                whole(2, 64, 256),
            ],
            out_specs=[whole(8, 1024, 128), *[whole(8, 128)] * 4],
            scratch_shapes=[
                pltpu.VMEM((2, 256, 256), F32),
                pltpu.VMEM((256, 2048), BF16),
                pltpu.VMEM((256, 2048), BF16),
                pltpu.VMEM((2, 160, 128), F32),
                pltpu.VMEM((16, 1024), BF16),
            ],
        ),
        name="source_stage",
    )(pos, weights, owner_slot, ranks, stacked, turn_c, turn_p)


GROUP = 3
PAIR = 2
MOST_TILES = 96


def target_kernel(
    pos_ref, excl_ref, rank_ref, slot_at_ref, delta_hbm, piv_ref, excl_v, rank_v, out_ref,
    delta, pivots, points_x, points_y, sums, box_of, rows_x, parts, lines, tiles, base, run, sem,
):
    def fetch(j):
        return pltpu.make_async_copy(delta_hbm.at[j], delta.at[j], sem.at[j])

    for j in range(8):
        fetch(j).start()
    pos = pos_ref[0]
    lane = lax.broadcasted_iota(I32, (8, 128), 1)
    sub = lax.broadcasted_iota(I32, (8, 128), 0)
    sub32 = lax.broadcasted_iota(I32, (32, 128), 0).astype(F32)
    corner_x = 64 * (pos >> 2) - 1024
    turn_x = corner_x.astype(F32) * (1.0 / 2048)
    corner_y = (64 * ((pos & 3) * 8 + 2 * (sub & 3) + (sub >> 2)) - 1024).astype(F32)
    turn_y = corner_y * (1.0 / 2048)
    off_col = by_sublane(PARENT_OFF, lane)
    k_x = corner_x.astype(F32) + off_col
    k_sq_x = k_x * k_x

    for n in range(8):
        p = piv_ref[n * 16 : n * 16 + 16].reshape(128, 128).astype(F32)
        pivots[n] = jnp.transpose(p)[0:32, :]
    lane32 = lax.broadcasted_iota(I32, (32, 128), 1)

    def one_block(j, first_tile):
        e1, e2, half = j >> 2, (j >> 1) & 1, j & 1
        pick = e1 * 64 + 2 * (lane32 & 31) + e2
        p = lanes_of(pivots[half * 4], pick)
        for g in range(1, 4):
            p = jnp.where((lane32 >> 5) == g, lanes_of(pivots[half * 4 + g], pick), p)
        p = p.astype(I32)
        box_x = 2 * (half * 4 + (lane32 >> 5)) + e1
        box_y = 2 * (lane32 & 31) + e2
        points_x[...] = (32 * box_x + (p >> 5)).astype(F32)
        points_y[...] = (32 * box_y + (p & 31)).astype(F32)
        start_row = jnp.broadcast_to(excl_v[pl.ds(j, 1), :], (8, 128)).astype(F32)
        end_row = start_row + jnp.broadcast_to(rank_v[pl.ds(j, 1), :], (8, 128)).astype(F32)
        ends_low = lanes_of(end_row, 8 * sub + 7)
        ends_high = lanes_of(end_row, 64 + 8 * sub + 7)
        ends_in = lanes_of(end_row, jnp.minimum(8 * lane + sub, 127))
        base[j] = first_tile
        n_tiles = (excl_ref[j, 127] + rank_ref[j, 127] + 127) >> 7

        def one_tile(k, tile):
            run[tile] = j
            row = (k * 128 + lane).astype(F32)
            ahead = jnp.where(ends_low <= row, 1.0, 0.0) + jnp.where(ends_high <= row, 1.0, 0.0)
            group = jnp.minimum(jnp.sum(ahead, axis=0, keepdims=True), 15.0)
            group = jnp.broadcast_to(group, (8, 128))
            inner = jnp.where(lanes_of(ends_in, group.astype(I32)) <= row, 1.0, 0.0)
            inner = jnp.broadcast_to(jnp.sum(inner, axis=0, keepdims=True), (8, 128))
            idx = jnp.minimum(8.0 * group + inner, 127.0).astype(I32)
            place = row - lanes_of(start_row, idx)
            idx32 = jnp.concatenate([idx] * 4)
            mine = sub32 == jnp.concatenate([place] * 4)
            got_x = jnp.where(mine, lanes_of(points_x[...], idx32), 0.0)
            got_y = jnp.where(mine, lanes_of(points_y[...], idx32), 0.0)
            h_x = jnp.broadcast_to(jnp.sum(got_x, axis=0, keepdims=True), (8, 128))
            h_y = jnp.broadcast_to(jnp.sum(got_y, axis=0, keepdims=True), (8, 128))
            sq_x, sq_y = speeds(h_x * (1.0 / 256), h_y * (1.0 / 256))
            x, y = h_x * (1.0 / 2048), h_y * (1.0 / 2048)
            box_of[tile] = idx
            rows_x[tile, 0:8, :] = sq_x * k_sq_x
            rows_x[tile, 8:16, :] = wrap(h_x * turn_x) + x * off_col
            whole_y = wrap(h_y * turn_y)
            for t2 in range(8):
                k_y = corner_y + PARENT_OFF[t2]
                parts[tile, t2] = sq_y * (k_y * k_y)
                lines[tile, t2] = wrap(whole_y + y * PARENT_OFF[t2])

        def one_group(i, _):
            for h in range(GROUP):
                one_tile(i * GROUP + h, first_tile + i * GROUP + h)
            return 0

        lax.fori_loop(0, (n_tiles + GROUP - 1) // GROUP, one_group, 0)
        fetch(j).wait()
        total_re = jnp.zeros((8, 128), F32)
        total_im = jnp.zeros((8, 128), F32)
        for t in range(64):
            total_re = total_re + delta[j, t * 8 : t * 8 + 8, :]
            total_im = total_im + delta[j, 512 + t * 8 : 520 + t * 8, :]
        sums[j, 0:8, :] = total_re
        sums[j, 8:16, :] = total_im
        return first_tile + n_tiles

    n_all = lax.fori_loop(0, 8, one_block, 0)

    def one_sum(tile):
        j = run[tile]
        idx = box_of[tile]
        acc_re = lanes_of(sums[j, 0:8, :], idx)
        acc_im = lanes_of(sums[j, 8:16, :], idx)
        for t1 in range(8):
            part_x = jnp.broadcast_to(rows_x[tile, t1 : t1 + 1, :], (8, 128))
            line_x = jnp.broadcast_to(rows_x[tile, 8 + t1 : 9 + t1, :], (8, 128))
            for t2 in range(8):
                t = t1 * 8 + t2
                d_re = lanes_of(delta[j, t * 8 : t * 8 + 8, :], idx)
                d_im = lanes_of(delta[j, 512 + t * 8 : 520 + t * 8, :], idx)
                d, s = sine_parts(
                    root(part_x + parts[tile, t2]) + (line_x + lines[tile, t2]), SIN_C
                )
                acc_re = acc_re - (d * d_re + s * d_im)
                acc_im = acc_im + (s * d_re - d * d_im)
        acc_re = acc_re + pltpu.roll(acc_re, 4, 0)
        acc_im = acc_im + pltpu.roll(acc_im, 4, 0)
        return jnp.where(sub < 4, acc_re, acc_im)

    def one_pair(i, _):
        at = [jnp.minimum(i * PAIR + h, n_all - 1) for h in range(PAIR)]
        done = [one_sum(tile) for tile in at]
        for tile, value in zip(at, done):
            tiles[tile] = value
        return 0

    lax.fori_loop(0, (n_all + PAIR - 1) // PAIR, one_pair, 0)

    def one_owner(o, _):
        for part in range(2):
            out = jnp.zeros((8, 128), F32)
            for q in range(4):
                at = slot_at_ref[o >> 4, (o & 15) * 8 + part * 4 + q]
                place = base[at >> 13] * 128 + (at & 8191)
                tile = place >> 7
                off = place & 127
                joined = jnp.where(lane >= off, tiles[tile], tiles[tile + 1])
                joined = pltpu.roll(joined, (q * 32 - off) & 127, 1)
                out = joined if q == 0 else jnp.where((lane >> 5) == q, joined, out)
            out_ref[o, :, part * 128 : part * 128 + 128] = out
        return 0

    lax.fori_loop(0, 128, one_owner, 0, unroll=4)


def target_stage(pos, excl, rank, slot_at, delta, piv):
    smem = pl.BlockSpec(memory_space=pltpu.SMEM)
    vmem = pl.BlockSpec(memory_space=pltpu.VMEM)
    hbm = pl.BlockSpec(memory_space=pl.ANY)
    return pl.pallas_call(
        target_kernel,
        out_shape=jax.ShapeDtypeStruct((128, 8, 256), F32),
        in_specs=[smem, smem, smem, smem, hbm, vmem, vmem, vmem],
        out_specs=vmem,
        scratch_shapes=[
            pltpu.VMEM((8, 1024, 128), F32),
            pltpu.VMEM((8, 32, 128), F32),
            pltpu.VMEM((32, 128), F32),
            pltpu.VMEM((32, 128), F32),
            pltpu.VMEM((8, 16, 128), F32),
            pltpu.VMEM((MOST_TILES, 8, 128), I32),
            pltpu.VMEM((MOST_TILES, 16, 128), F32),
            pltpu.VMEM((MOST_TILES, 8, 8, 128), F32),
            pltpu.VMEM((MOST_TILES, 8, 8, 128), F32),
            pltpu.VMEM((MOST_TILES, 8, 128), F32),
            pltpu.SMEM((8,), I32),
            pltpu.SMEM((MOST_TILES,), I32),
            pltpu.SemaphoreType.DMA((8,)),
        ],
        name="target_stage",
    )(pos, excl, rank, slot_at, delta, piv, excl, rank)


def owner_kernel(pos_ref, rank_ref, in_ref, out_ref, gathered):
    pos = pos_ref[0]
    sub = lax.broadcasted_iota(I32, (8, 256), 0)
    for p1 in range(16):
        part = [in_ref[p1 * 8 + q] + in_ref[p1 * 8 + 4 + q] for q in range(4)]
        for m in range(2):
            even, odd = part[2 * m], part[2 * m + 1]
            row = p1 * 16 + m * 8
            gathered[0, row : row + 8, :] = jnp.where(sub < 4, even, pltpu.roll(odd, 4, 0))
            gathered[1, row : row + 8, :] = jnp.where(sub < 4, pltpu.roll(even, 4, 0), odd)
    i = lax.broadcasted_iota(I32, (32, 256), 0)
    for z in range(2):
        rows = jnp.transpose(gathered[z])
        for k in range(8):
            live = i < rank_ref[pos >> 4, (pos & 15) * 8 + k]
            out_ref[z, :, k, :] = jnp.where(live, rows[k * 32 : k * 32 + 32], 0.0)


def owner_stage(pos, rank, received):
    smem = pl.BlockSpec(memory_space=pltpu.SMEM)
    vmem = pl.BlockSpec(memory_space=pltpu.VMEM)
    return pl.pallas_call(
        owner_kernel,
        out_shape=jax.ShapeDtypeStruct((2, 32, 8, 256), F32),
        in_specs=[smem, smem, vmem],
        out_specs=vmem,
        scratch_shapes=[pltpu.VMEM((2, 256, 256), F32)],
        name="owner_stage",
    )(pos, rank, received)


def local(child_weights, pivots, ranks, owner_slot):
    pos = lax.axis_index("grp") * lax.axis_size("dev") + lax.axis_index("dev")
    pos = pos.astype(I32).reshape(1)
    spread = jnp.broadcast_to(jnp.pad(pivots, ((0, 0), (0, 96)))[None], (128, 8, 128))
    all_pivots = lax.all_to_all(spread, AXES, split_axis=0, concat_axis=0, tiled=True)
    at = owner_slot.reshape(8, 128)
    weights = child_weights.reshape(2, 8, 256, 256)
    delta, excl, rank, slot_at, slot_rank = source_stage(pos, weights, at, ranks.reshape(8, 128))
    send = target_stage(pos, excl, rank, slot_at, delta, all_pivots)
    received = lax.all_to_all(send, AXES, split_axis=0, concat_axis=0, tiled=True)
    return owner_stage(pos, slot_rank, received)


def solution(mesh):
    in_specs = (P(None, AXES, None, None, None), P(AXES, None), P(), P())
    out_specs = P(None, None, AXES, None)
    return jax.shard_map(local, mesh=mesh, in_specs=in_specs, out_specs=out_specs, check_vma=False)
```

```python
import numpy as np

import jax
import jax.numpy as jnp
from jax import lax
from jax.experimental import pallas as pl
from jax.experimental.pallas import tpu as pltpu
from jax.sharding import PartitionSpec as P

AXES = ("grp", "dev")
F32 = jnp.float32
BF16 = jnp.bfloat16
I32 = jnp.int32

SIN_C = (2.6417391300201416, -1.0859273672103882, 0.13053695857524872)
SIN_FINE = (2.641753911972046, -1.0863757133483887, 0.1339970976114273, -0.007720405701547861)
ROOT2 = 1.4142135623730951
ROOT8 = 2.8284271247461903


def _f32(x):
    return np.float32(x)


CHEB = [_f32(np.cos(np.pi * (2 * j + 1) / 16.0)) for j in range(8)]
PARENT_OFF = [float(_f32(31.5) + _f32(32.0) * c) for c in CHEB]
CHILD_OFF = [[float(_f32(32.0 * u + 15.5) + _f32(16.0) * c) for c in CHEB] for u in range(2)]


def interp_matrix():
    nodes = np.cos(np.pi * (2 * np.arange(8) + 1) / 16.0)
    halves = np.zeros((2, 8, 8))
    for u in range(2):
        points = u - 0.5 + 0.5 * nodes
        for t in range(8):
            value = np.ones(8)
            for s in range(8):
                if s != t:
                    value = value * (points - nodes[s]) / (nodes[t] - nodes[s])
            halves[u, t] = value
    full = np.einsum("uaj,vbk->abuvjk", halves, halves).reshape(64, 256)
    return full.astype(np.float32)


def class_turns(off_x, off_y, sign):
    lane = np.arange(256)
    a, b = lane // 128, (lane % 32) // 4
    cycles = (np.outer(off_x, a) + np.outer(off_y, b)) / 8.0
    angle = sign * 2.0 * np.pi * (cycles % 1.0)
    return np.stack([np.cos(angle), np.sin(angle)]).astype(np.float32)


def wrap(x):
    return x - jnp.round(x)


def sine_parts(phase, coef):
    r = wrap(phase)
    z = r * r
    s = coef[-1]
    for c in coef[-2::-1]:
        s = s * z + c
    s = s * r
    q = s * s
    w = ROOT8 - q
    v = w * lax.rsqrt(w)
    return q * w, (s * v) * (ROOT2 - q)


def cos_sin(phase, coef=SIN_C):
    d, s = sine_parts(phase, coef)
    return 1.0 - d, s


def root(x):
    return x * lax.rsqrt(x)


def speeds(turn_x, turn_y):
    sub = lax.broadcasted_iota(I32, turn_x.shape, 0)
    c, s = cos_sin(jnp.where(sub < 4, turn_x, turn_y), SIN_FINE)
    c1 = (2.0 + s * pltpu.roll(s, 4, 0)) * 0.0625
    c2 = (2.0 + c * pltpu.roll(c, 4, 0)) * 0.0625
    return c1 * c1, c2 * c2


def split(x):
    hi = x.astype(BF16)
    return hi, (x - hi.astype(F32)).astype(BF16)


def by_sublane(values, like):
    sub = lax.broadcasted_iota(I32, like.shape, 0)
    out = jnp.full(like.shape, values[0], F32)
    for s in range(1, 8):
        out = jnp.where(sub == s, values[s], out)
    return out


def lanes_of(x, idx):
    return jnp.take_along_axis(x, idx, axis=1)


NT = (((1,), (1,)), ((), ()))


def source_kernel(
    pos_ref, w_ref, os_ref, ranks_ref, tab_ref, turn_c, turn_p,
    out_ref, excl_ref, rank_ref, slot_tile_ref, slot_off_ref, slot_rank_ref,
    w_turned, wave, labels,
):
    step = pl.program_id(0)
    pos = pos_ref[0]
    lane = lax.broadcasted_iota(I32, (8, 128), 1)
    sub = lax.broadcasted_iota(I32, (8, 128), 0)

    @pl.when(step == 0)
    def _():
        ranks = ranks_ref[...].astype(F32)
        owners = os_ref[...].astype(F32)
        rank8 = jnp.zeros((8, 128), F32)
        at_row = []
        for n in range(8):
            e1, e2, half = n // 4, (n // 2) % 2, n % 2
            idx = e1 * 64 + 2 * (lane % 32) + e2
            mine = sub == 4 * half + lane // 32
            at_row.append(
                jnp.sum(jnp.where(mine, lanes_of(owners, idx), 0.0), axis=0, keepdims=True)
            )
            rk = jnp.sum(jnp.where(mine, lanes_of(ranks, idx), 0.0), axis=0, keepdims=True)
            rank8 = jnp.where(sub == n, jnp.broadcast_to(rk, (8, 128)), rank8)
        upto = (
            lax.broadcasted_iota(I32, (128, 128), 0) <= lax.broadcasted_iota(I32, (128, 128), 1)
        )
        upto = jnp.where(upto, 1.0, 0.0).astype(BF16)
        excl8 = jnp.dot(rank8.astype(BF16), upto, preferred_element_type=F32) - rank8
        rank_ref[...] = rank8.astype(I32)
        excl_ref[...] = excl8.astype(I32)
        live = lanes_of(excl8 + rank8, jnp.full((8, 128), 127, I32)).astype(I32)
        n_tiles = (live + 127) >> 7
        first = jnp.zeros((1, 128), I32)
        row = lax.broadcasted_iota(I32, (16, 128), 0)
        for n in range(8):
            rk = jnp.broadcast_to(rank8[n : n + 1], (16, 128))
            ahead = jnp.broadcast_to(excl8[n : n + 1], (16, 128)).astype(I32)
            high, low = (ahead >> 6).astype(F32), (ahead & 63).astype(F32)
            label = jnp.where(row == 2, high, jnp.where(row == 3, low, 0.0))
            start = jnp.broadcast_to(first.astype(F32), (16, 128))
            label = jnp.where(row == 0, rk, jnp.where(row == 1, start, label))
            first = first + n_tiles[n : n + 1]
            labels[:, n * 128 : n * 128 + 128] = label.astype(BF16)
        for j in range(8):
            slot = lax.broadcasted_iota(I32, (128, 128), 0).astype(F32) + j * 128.0
            got = jnp.zeros((16, 128), F32)
            for n in range(8):
                hit = jnp.where(slot == jnp.broadcast_to(at_row[n], (128, 128)), 1.0, 0.0)
                got = got + lax.dot_general(
                    labels[:, n * 128 : n * 128 + 128], hit.astype(BF16), NT,
                    preferred_element_type=F32,
                )
            slot_rank_ref[j : j + 1, :] = got[0:1].astype(I32)
            at = (got[1:2] * 128.0 + got[2:3] * 64.0 + got[3:4]).astype(I32)
            slot_tile_ref[j : j + 1, :] = at >> 7
            slot_off_ref[j : j + 1, :] = at & 127

    box = 2 * (step % 4) + step // 4
    corner_xf = (64 * (pos // 4) - 1024).astype(F32)
    corner_yf = (64 * ((pos % 4) * 8 + box) - 1024).astype(F32)
    h_x = 64 * ((lane % 64) // 8) + 31
    h_y = 64 * (lane % 8) + 31
    h_xf, h_yf = h_x.astype(F32), h_y.astype(F32)
    sq_x, sq_y = speeds(h_xf * (1.0 / 512), h_yf * (1.0 / 512))
    x, y = h_xf * (1.0 / 4096), h_yf * (1.0 / 4096)
    high = lane >= 64

    off_y = jnp.where(high, by_sublane(CHILD_OFF[1], lane), by_sublane(CHILD_OFF[0], lane))
    k_y = corner_yf + off_y
    part_y, line_y = sq_y * (k_y * k_y), y * off_y
    for u in range(2):
        for j1 in range(8):
            off_x = CHILD_OFF[u][j1]
            k_x = corner_xf + off_x
            c, s = cos_sin(root(sq_x * (k_x * k_x) + part_y) + (x * off_x + line_y))
            wave[0, (u * 8 + j1) * 8 : (u * 8 + j1) * 8 + 8, :] = c
            wave[1, (u * 8 + j1) * 8 : (u * 8 + j1) * 8 + 8, :] = s
    off_y = by_sublane(PARENT_OFF, lane)
    k_y = corner_yf + off_y
    part_y, line_y = sq_y * (k_y * k_y), y * off_y
    for m in range(4):
        off_x = jnp.where(high, PARENT_OFF[2 * m + 1], PARENT_OFF[2 * m])
        k_x = corner_xf + off_x
        c, s = cos_sin(root(sq_x * (k_x * k_x) + part_y) + (x * off_x + line_y))
        wave[0, 128 + m * 8 : 136 + m * 8, :] = c
        wave[1, 128 + m * 8 : 136 + m * 8, :] = s

    for part in range(4):
        rows = slice(part * 64, part * 64 + 64)
        w_re, w_im = w_ref[0, 0, rows, :], w_ref[1, 0, rows, :]
        t_re, t_im = turn_c[0, rows, :], turn_c[1, rows, :]
        w_turned[0, rows, :] = w_re * t_re - w_im * t_im
        w_turned[1, rows, :] = w_re * t_im + w_im * t_re

    for e in range(4):
        e1, e2 = e // 2, e % 2
        pick = (2 * (lane // 32) + e1) * 8 + 2 * (lane % 4) + e2
        high_parts = [[], [], [], []]
        low_parts = [[], [], [], []]
        for u in range(2):
            for v in range(2):
                idx = pick + v * 64
                for g in range(4):
                    base = (u * 8 + 2 * g) * 8
                    c = jnp.concatenate(
                        [lanes_of(wave[0, base + 8 * i : base + 8 * i + 8, :], idx) for i in (0, 1)]
                    )
                    s = jnp.concatenate(
                        [lanes_of(wave[1, base + 8 * i : base + 8 * i + 8, :], idx) for i in (0, 1)]
                    )
                    at = (u * 2 + v) * 64 + g * 16
                    rows = slice(at, at + 16)
                    for half in range(2):
                        w_re = w_turned[0, rows, half * 128 : half * 128 + 128]
                        w_im = w_turned[1, rows, half * 128 : half * 128 + 128]
                        for z, value in (
                            (half, w_re * c + w_im * s),
                            (2 + half, w_im * c - w_re * s),
                        ):
                            hi, lo = split(value)
                            high_parts[z].append(hi)
                            low_parts[z].append(lo)
        mod_hi = jnp.concatenate([jnp.concatenate(p, axis=0) for p in high_parts], axis=1)
        mod_lo = jnp.concatenate([jnp.concatenate(p, axis=0) for p in low_parts], axis=1)
        first = jnp.dot(tab_ref[...], mod_hi, preferred_element_type=F32)
        second = jnp.dot(tab_ref[0:64, :], mod_lo, preferred_element_type=F32)
        interp = first[0:64] + (first[64:128] + second)
        c = jnp.concatenate(
            [
                lanes_of(wave[0, 128 + (t // 2) * 8 : 136 + (t // 2) * 8, :], pick + (t % 2) * 64)
                for t in range(8)
            ]
        )
        s = jnp.concatenate(
            [
                lanes_of(wave[1, 128 + (t // 2) * 8 : 136 + (t // 2) * 8, :], pick + (t % 2) * 64)
                for t in range(8)
            ]
        )
        for half in range(2):
            i_re = interp[:, half * 128 : half * 128 + 128]
            i_im = interp[:, half * 128 + 256 : half * 128 + 384]
            t_re = turn_p[0, :, half * 128 : half * 128 + 128]
            t_im = turn_p[1, :, half * 128 : half * 128 + 128]
            g_re = i_re * t_re - i_im * t_im
            g_im = i_re * t_im + i_im * t_re
            out_ref[0, e * 2 + half, 0:64, :] = g_re * c - g_im * s
            out_ref[0, e * 2 + half, 64:128, :] = g_re * s + g_im * c


def source_stage(pos, weights, owner_slot, ranks):
    table = interp_matrix()
    hi = table.astype(jnp.bfloat16)
    lo = (table - hi.astype(np.float32)).astype(jnp.bfloat16)
    stacked = jnp.asarray(np.concatenate([hi, lo], axis=0))
    child = np.array(CHILD_OFF)
    row = np.arange(256)
    off_x = child[row // 128, (row // 8) % 8]
    off_y = child[(row // 64) % 2, row % 8]
    parent = np.array(PARENT_OFF)
    turn_c = jnp.asarray(class_turns(off_x, off_y, -1.0))
    turn_p = jnp.asarray(class_turns(parent[row[:64] // 8], parent[row[:64] % 8], 1.0))

    def whole(*shape):
        return pl.BlockSpec(shape, lambda g, p: (0,) * len(shape))

    return pl.pallas_call(
        source_kernel,
        out_shape=[
            jax.ShapeDtypeStruct((8, 8, 128, 128), F32),
            *[jax.ShapeDtypeStruct((8, 128), I32)] * 5,
        ],
        grid_spec=pltpu.PrefetchScalarGridSpec(
            num_scalar_prefetch=1,
            grid=(8,),
            in_specs=[
                pl.BlockSpec((2, 1, 256, 256), lambda g, p: (0, 2 * (g % 4) + g // 4, 0, 0)),
                whole(8, 128),
                whole(8, 128),
                whole(128, 256),
                whole(2, 256, 256),
                whole(2, 64, 256),
            ],
            out_specs=[pl.BlockSpec((1, 8, 128, 128), lambda g, p: (g, 0, 0, 0)), *[whole(8, 128)] * 5],
            scratch_shapes=[
                pltpu.VMEM((2, 256, 256), F32),
                pltpu.VMEM((2, 160, 128), F32),
                pltpu.VMEM((16, 1024), BF16),
            ],
        ),
        name="source_stage",
    )(pos, weights, owner_slot, ranks, stacked, turn_c, turn_p)


GROUP = 4
PAIR = 2
MOST_TILES = 96


def target_kernel(
    pos_ref, excl_ref, rank_ref, slot_tile, slot_off, delta_hbm, piv_ref, excl_v, rank_v, out_ref,
    delta, pivots, points_x, points_y, edges, sums, box_of, rows_x, parts, lines, tiles, run, place_of, sem,
):
    def fetch(j, b):
        return pltpu.make_async_copy(delta_hbm.at[b, j], delta.at[j, :, b, :], sem.at[j, b])

    for j in range(8):
        for b in range(8):
            fetch(j, b).start()
    pos = pos_ref[0]
    lane = lax.broadcasted_iota(I32, (8, 128), 1)
    sub = lax.broadcasted_iota(I32, (8, 128), 0)
    sub32 = lax.broadcasted_iota(I32, (32, 128), 0).astype(F32)
    corner_x = 64 * (pos >> 2) - 1024
    turn_x = corner_x.astype(F32) * (1.0 / 2048)
    corner_y = (64 * ((pos & 3) * 8 + 2 * (sub & 3) + (sub >> 2)) - 1024).astype(F32)
    turn_y = corner_y * (1.0 / 2048)
    off_col = by_sublane(PARENT_OFF, lane)
    k_x = corner_x.astype(F32) + off_col
    k_sq_x = k_x * k_x

    for n in range(8):
        p = piv_ref[n * 16 : n * 16 + 16].reshape(128, 128).astype(F32)
        pivots[n] = jnp.transpose(p)[0:32, :]
    lane32 = lax.broadcasted_iota(I32, (32, 128), 1)

    def one_block(j, first_tile):
        e1, e2, half = j >> 2, (j >> 1) & 1, j & 1
        pick = e1 * 64 + 2 * (lane32 & 31) + e2
        p = lanes_of(pivots[half * 4], pick)
        for g in range(1, 4):
            p = jnp.where((lane32 >> 5) == g, lanes_of(pivots[half * 4 + g], pick), p)
        p = p.astype(I32)
        box_x = 2 * (half * 4 + (lane32 >> 5)) + e1
        box_y = 2 * (lane32 & 31) + e2
        points_x[j] = (32 * box_x + (p >> 5)).astype(F32)
        points_y[j] = (32 * box_y + (p & 31)).astype(F32)
        start_row = jnp.broadcast_to(excl_v[pl.ds(j, 1), :], (8, 128)).astype(F32)
        end_row = start_row + jnp.broadcast_to(rank_v[pl.ds(j, 1), :], (8, 128)).astype(F32)
        edges[j, 0:8, :] = lanes_of(end_row, 8 * sub + 7)
        edges[j, 8:16, :] = lanes_of(end_row, 64 + 8 * sub + 7)
        edges[j, 16:24, :] = lanes_of(end_row, jnp.minimum(8 * lane + sub, 127))
        edges[j, 24:32, :] = start_row
        n_tiles = (excl_ref[j, 127] + rank_ref[j, 127] + 127) >> 7

        def note(k, _):
            run[first_tile + k] = j
            place_of[first_tile + k] = k * 128
            return 0

        lax.fori_loop(0, n_tiles, note, 0)
        for b in range(8):
            fetch(j, b).wait()
        total_re = jnp.zeros((8, 128), F32)
        total_im = jnp.zeros((8, 128), F32)
        for t in range(64):
            total_re = total_re + delta[j, t]
            total_im = total_im + delta[j, 64 + t]
        sums[j, 0:8, :] = total_re
        sums[j, 8:16, :] = total_im
        return first_tile + n_tiles

    n_all = lax.fori_loop(0, 8, one_block, 0)

    def one_tile(tile):
        j = run[tile]
        row = (place_of[tile] + lane).astype(F32)
        ahead = jnp.where(edges[j, 0:8, :] <= row, 1.0, 0.0)
        ahead = ahead + jnp.where(edges[j, 8:16, :] <= row, 1.0, 0.0)
        group = jnp.minimum(jnp.sum(ahead, axis=0, keepdims=True), 15.0)
        group = jnp.broadcast_to(group, (8, 128))
        inner = jnp.where(lanes_of(edges[j, 16:24, :], group.astype(I32)) <= row, 1.0, 0.0)
        inner = jnp.broadcast_to(jnp.sum(inner, axis=0, keepdims=True), (8, 128))
        idx = jnp.minimum(8.0 * group + inner, 127.0).astype(I32)
        place = row - lanes_of(edges[j, 24:32, :], idx)
        idx32 = jnp.concatenate([idx] * 4)
        mine = sub32 == jnp.concatenate([place] * 4)
        got_x = jnp.where(mine, lanes_of(points_x[j], idx32), 0.0)
        got_y = jnp.where(mine, lanes_of(points_y[j], idx32), 0.0)
        h_x = jnp.broadcast_to(jnp.sum(got_x, axis=0, keepdims=True), (8, 128))
        h_y = jnp.broadcast_to(jnp.sum(got_y, axis=0, keepdims=True), (8, 128))
        sq_x, sq_y = speeds(h_x * (1.0 / 256), h_y * (1.0 / 256))
        x, y = h_x * (1.0 / 2048), h_y * (1.0 / 2048)
        whole_y = wrap(h_y * turn_y)
        part, line = [], []
        for off in PARENT_OFF:
            k_y = corner_y + off
            part.append(sq_y * (k_y * k_y))
            line.append(wrap(whole_y + y * off))
        return idx, sq_x * k_sq_x, wrap(h_x * turn_x) + x * off_col, part, line

    def one_group(i, _):
        at = [jnp.minimum(i * GROUP + h, n_all - 1) for h in range(GROUP)]
        found = [one_tile(tile) for tile in at]
        for tile, (idx, part_x, line_x, part, line) in zip(at, found):
            box_of[tile] = idx
            rows_x[tile, 0:8, :] = part_x
            rows_x[tile, 8:16, :] = line_x
            for t2 in range(8):
                parts[tile, t2] = part[t2]
                lines[tile, t2] = line[t2]
        return 0

    lax.fori_loop(0, (n_all + GROUP - 1) // GROUP, one_group, 0)

    def one_sum(tile):
        j = run[tile]
        idx = box_of[tile]
        acc_re = lanes_of(sums[j, 0:8, :], idx)
        acc_im = lanes_of(sums[j, 8:16, :], idx)
        for t1 in range(8):
            part_x = jnp.broadcast_to(rows_x[tile, t1 : t1 + 1, :], (8, 128))
            line_x = jnp.broadcast_to(rows_x[tile, 8 + t1 : 9 + t1, :], (8, 128))
            for t2 in range(8):
                t = t1 * 8 + t2
                d_re = lanes_of(delta[j, t], idx)
                d_im = lanes_of(delta[j, 64 + t], idx)
                d, s = sine_parts(
                    root(part_x + parts[tile, t2]) + (line_x + lines[tile, t2]), SIN_C
                )
                acc_re = acc_re - (d * d_re + s * d_im)
                acc_im = acc_im + (s * d_re - d * d_im)
        acc_re = acc_re + pltpu.roll(acc_re, 4, 0)
        acc_im = acc_im + pltpu.roll(acc_im, 4, 0)
        return jnp.where(sub < 4, acc_re, acc_im)

    def one_pair(i, _):
        at = [jnp.minimum(i * PAIR + h, n_all - 1) for h in range(PAIR)]
        done = [one_sum(tile) for tile in at]
        for tile, value in zip(at, done):
            tiles[tile] = value
        return 0

    lax.fori_loop(0, (n_all + PAIR - 1) // PAIR, one_pair, 0)

    def one_owner(o, _):
        for part in range(2):
            out = jnp.zeros((8, 128), F32)
            for q in range(4):
                tile = slot_tile[o * 8 + part * 4 + q]
                off = slot_off[o * 8 + part * 4 + q]
                joined = jnp.where(lane >= off, tiles[tile], tiles[tile + 1])
                joined = pltpu.roll(joined, (q * 32 + 128 - off) & 127, 1)
                out = joined if q == 0 else jnp.where((lane >> 5) == q, joined, out)
            out_ref[o, :, part * 128 : part * 128 + 128] = out
        return 0

    lax.fori_loop(0, 128, one_owner, 0, unroll=4)


def target_stage(pos, excl, rank, slot_tile, slot_off, delta, piv):
    smem = pl.BlockSpec(memory_space=pltpu.SMEM)
    vmem = pl.BlockSpec(memory_space=pltpu.VMEM)
    hbm = pl.BlockSpec(memory_space=pl.ANY)
    return pl.pallas_call(
        target_kernel,
        out_shape=jax.ShapeDtypeStruct((128, 8, 256), F32),
        in_specs=[smem, smem, smem, smem, smem, hbm, vmem, vmem, vmem],
        out_specs=vmem,
        scratch_shapes=[
            pltpu.VMEM((8, 128, 8, 128), F32),
            pltpu.VMEM((8, 32, 128), F32),
            pltpu.VMEM((8, 32, 128), F32),
            pltpu.VMEM((8, 32, 128), F32),
            pltpu.VMEM((8, 32, 128), F32),
            pltpu.VMEM((8, 16, 128), F32),
            pltpu.VMEM((MOST_TILES, 8, 128), I32),
            pltpu.VMEM((MOST_TILES, 16, 128), F32),
            pltpu.VMEM((MOST_TILES, 8, 8, 128), F32),
            pltpu.VMEM((MOST_TILES, 8, 8, 128), F32),
            pltpu.VMEM((MOST_TILES, 8, 128), F32),
            pltpu.SMEM((MOST_TILES,), I32),
            pltpu.SMEM((MOST_TILES,), I32),
            pltpu.SemaphoreType.DMA((8, 8)),
        ],
        name="target_stage",
    )(
        pos, excl, rank, slot_tile.reshape(1024), slot_off.reshape(1024), delta, piv, excl, rank
    )


def owner_kernel(pos_ref, rank_ref, in_ref, out_ref, gathered):
    pos = pos_ref[0]
    sub = lax.broadcasted_iota(I32, (8, 256), 0)
    for p1 in range(16):
        part = [in_ref[p1 * 8 + q] + in_ref[p1 * 8 + 4 + q] for q in range(4)]
        for m in range(2):
            even, odd = part[2 * m], part[2 * m + 1]
            row = p1 * 16 + m * 8
            gathered[0, row : row + 8, :] = jnp.where(sub < 4, even, pltpu.roll(odd, 4, 0))
            gathered[1, row : row + 8, :] = jnp.where(sub < 4, pltpu.roll(even, 4, 0), odd)
    i = lax.broadcasted_iota(I32, (32, 256), 0)
    for z in range(2):
        rows = jnp.transpose(gathered[z])
        for k in range(8):
            live = i < rank_ref[pos >> 4, (pos & 15) * 8 + k]
            out_ref[z, :, k, :] = jnp.where(live, rows[k * 32 : k * 32 + 32], 0.0)


def owner_stage(pos, rank, received):
    smem = pl.BlockSpec(memory_space=pltpu.SMEM)
    vmem = pl.BlockSpec(memory_space=pltpu.VMEM)
    return pl.pallas_call(
        owner_kernel,
        out_shape=jax.ShapeDtypeStruct((2, 32, 8, 256), F32),
        in_specs=[smem, smem, vmem],
        out_specs=vmem,
        scratch_shapes=[pltpu.VMEM((2, 256, 256), F32)],
        name="owner_stage",
    )(pos, rank, received)


def local(child_weights, pivots, ranks, owner_slot):
    pos = lax.axis_index("grp") * lax.axis_size("dev") + lax.axis_index("dev")
    pos = pos.astype(I32).reshape(1)
    wide = jnp.pad(pivots, ((0, 0), (0, 96)))
    spread = jnp.where(lax.broadcasted_iota(I32, (128, 8, 128), 2) < 32, wide[None], 0)
    all_pivots = lax.all_to_all(spread, AXES, split_axis=0, concat_axis=0, tiled=True)
    at = owner_slot.reshape(8, 128)
    weights = child_weights.reshape(2, 8, 256, 256)
    delta, excl, rank, slot_tile, slot_off, slot_rank = source_stage(
        pos, weights, at, ranks.reshape(8, 128)
    )
    send = target_stage(pos, excl, rank, slot_tile, slot_off, delta, all_pivots)
    received = lax.all_to_all(send, AXES, split_axis=0, concat_axis=0, tiled=True)
    return owner_stage(pos, slot_rank, received)


def solution(mesh):
    in_specs = (P(None, AXES, None, None, None), P(AXES, None), P(), P())
    out_specs = P(None, None, AXES, None)
    return jax.shard_map(local, mesh=mesh, in_specs=in_specs, out_specs=out_specs, check_vma=False)
```

```python
import numpy as np

import jax
import jax.numpy as jnp
from jax import lax
from jax.experimental import pallas as pl
from jax.experimental.pallas import tpu as pltpu
from jax.sharding import PartitionSpec as P

AXES = ("grp", "dev")
F32 = jnp.float32
BF16 = jnp.bfloat16
I32 = jnp.int32

SIN_C = (2.6417391300201416, -1.0859273672103882, 0.13053695857524872)
SIN_FINE = (2.641753911972046, -1.0863757133483887, 0.1339970976114273, -0.007720405701547861)
ROOT2 = 1.4142135623730951
ROOT8 = 2.8284271247461903


def _f32(x):
    return np.float32(x)


CHEB = [_f32(np.cos(np.pi * (2 * j + 1) / 16.0)) for j in range(8)]
PARENT_OFF = [float(_f32(31.5) + _f32(32.0) * c) for c in CHEB]
CHILD_OFF = [[float(_f32(32.0 * u + 15.5) + _f32(16.0) * c) for c in CHEB] for u in range(2)]


def interp_matrix():
    nodes = np.cos(np.pi * (2 * np.arange(8) + 1) / 16.0)
    halves = np.zeros((2, 8, 8))
    for u in range(2):
        points = u - 0.5 + 0.5 * nodes
        for t in range(8):
            value = np.ones(8)
            for s in range(8):
                if s != t:
                    value = value * (points - nodes[s]) / (nodes[t] - nodes[s])
            halves[u, t] = value
    full = np.einsum("uaj,vbk->abuvjk", halves, halves).reshape(64, 256)
    return full.astype(np.float32)


def class_turns(off_x, off_y, sign):
    lane = np.arange(256)
    a, b = lane // 128, (lane % 32) // 4
    cycles = (np.outer(off_x, a) + np.outer(off_y, b)) / 8.0
    angle = sign * 2.0 * np.pi * (cycles % 1.0)
    return np.stack([np.cos(angle), np.sin(angle)]).astype(np.float32)


def wrap(x):
    return x - jnp.round(x)


def sine_parts(phase, coef):
    r = wrap(phase)
    z = r * r
    s = coef[-1]
    for c in coef[-2::-1]:
        s = s * z + c
    s = s * r
    q = s * s
    w = ROOT8 - q
    v = w * lax.rsqrt(w)
    return q * w, (s * v) * (ROOT2 - q)


def cos_sin(phase, coef=SIN_C):
    d, s = sine_parts(phase, coef)
    return 1.0 - d, s


def root(x):
    return x * lax.rsqrt(x)


def speeds(turn_x, turn_y):
    sub = lax.broadcasted_iota(I32, turn_x.shape, 0)
    c, s = cos_sin(jnp.where(sub < 4, turn_x, turn_y), SIN_FINE)
    c1 = (2.0 + s * pltpu.roll(s, 4, 0)) * 0.0625
    c2 = (2.0 + c * pltpu.roll(c, 4, 0)) * 0.0625
    return c1 * c1, c2 * c2


def split(x):
    hi = x.astype(BF16)
    return hi, (x - hi.astype(F32)).astype(BF16)


def by_sublane(values, like):
    sub = lax.broadcasted_iota(I32, like.shape, 0)
    out = jnp.full(like.shape, values[0], F32)
    for s in range(1, 8):
        out = jnp.where(sub == s, values[s], out)
    return out


def lanes_of(x, idx):
    return jnp.take_along_axis(x, idx, axis=1)


NT = (((1,), (1,)), ((), ()))


def source_kernel(
    pos_ref, w_ref, os_ref, ranks_ref, tab_ref, turn_c, turn_p,
    out_ref, excl_ref, rank_ref, slot_tile_ref, slot_off_ref, slot_rank_ref,
    w_turned, wave, labels,
):
    step = pl.program_id(0)
    pos = pos_ref[0]
    lane = lax.broadcasted_iota(I32, (8, 128), 1)
    sub = lax.broadcasted_iota(I32, (8, 128), 0)

    @pl.when(step == 0)
    def _():
        ranks = ranks_ref[...].astype(F32)
        owners = os_ref[...].astype(F32)
        rank8 = jnp.zeros((8, 128), F32)
        at_row = []
        for n in range(8):
            e1, e2, half = n // 4, (n // 2) % 2, n % 2
            idx = e1 * 64 + 2 * (lane % 32) + e2
            mine = sub == 4 * half + lane // 32
            at_row.append(
                jnp.sum(jnp.where(mine, lanes_of(owners, idx), 0.0), axis=0, keepdims=True)
            )
            rk = jnp.sum(jnp.where(mine, lanes_of(ranks, idx), 0.0), axis=0, keepdims=True)
            rank8 = jnp.where(sub == n, jnp.broadcast_to(rk, (8, 128)), rank8)
        upto = (
            lax.broadcasted_iota(I32, (128, 128), 0) <= lax.broadcasted_iota(I32, (128, 128), 1)
        )
        upto = jnp.where(upto, 1.0, 0.0).astype(BF16)
        excl8 = jnp.dot(rank8.astype(BF16), upto, preferred_element_type=F32) - rank8
        rank_ref[...] = rank8.astype(I32)
        excl_ref[...] = excl8.astype(I32)
        live = lanes_of(excl8 + rank8, jnp.full((8, 128), 127, I32)).astype(I32)
        n_tiles = (live + 127) >> 7
        first = jnp.zeros((1, 128), I32)
        row = lax.broadcasted_iota(I32, (16, 128), 0)
        for n in range(8):
            rk = jnp.broadcast_to(rank8[n : n + 1], (16, 128))
            ahead = jnp.broadcast_to(excl8[n : n + 1], (16, 128)).astype(I32)
            high, low = (ahead >> 6).astype(F32), (ahead & 63).astype(F32)
            label = jnp.where(row == 2, high, jnp.where(row == 3, low, 0.0))
            start = jnp.broadcast_to(first.astype(F32), (16, 128))
            label = jnp.where(row == 0, rk, jnp.where(row == 1, start, label))
            first = first + n_tiles[n : n + 1]
            labels[:, n * 128 : n * 128 + 128] = label.astype(BF16)
        for j in range(8):
            slot = lax.broadcasted_iota(I32, (128, 128), 0).astype(F32) + j * 128.0
            got = jnp.zeros((16, 128), F32)
            for n in range(8):
                hit = jnp.where(slot == jnp.broadcast_to(at_row[n], (128, 128)), 1.0, 0.0)
                got = got + lax.dot_general(
                    labels[:, n * 128 : n * 128 + 128], hit.astype(BF16), NT,
                    preferred_element_type=F32,
                )
            slot_rank_ref[j : j + 1, :] = got[0:1].astype(I32)
            at = (got[1:2] * 128.0 + got[2:3] * 64.0 + got[3:4]).astype(I32)
            slot_tile_ref[j : j + 1, :] = at >> 7
            slot_off_ref[j : j + 1, :] = at & 127

    corner_xf = (64 * (pos // 4) - 1024).astype(F32)
    h_x = 64 * ((lane % 64) // 8) + 31
    h_y = 64 * (lane % 8) + 31
    h_xf, h_yf = h_x.astype(F32), h_y.astype(F32)
    sq_x, sq_y = speeds(h_xf * (1.0 / 512), h_yf * (1.0 / 512))
    x, y = h_xf * (1.0 / 4096), h_yf * (1.0 / 4096)
    high = lane >= 64

    for box in range(2):
        corner_yf = (64 * ((pos % 4) * 8 + 2 * step + box) - 1024).astype(F32)
        off_y = jnp.where(high, by_sublane(CHILD_OFF[1], lane), by_sublane(CHILD_OFF[0], lane))
        k_y = corner_yf + off_y
        part_y, line_y = sq_y * (k_y * k_y), y * off_y
        for u in range(2):
            for j1 in range(8):
                off_x = CHILD_OFF[u][j1]
                k_x = corner_xf + off_x
                c, s = cos_sin(root(sq_x * (k_x * k_x) + part_y) + (x * off_x + line_y))
                wave[box, 0, (u * 8 + j1) * 8 : (u * 8 + j1) * 8 + 8, :] = c
                wave[box, 1, (u * 8 + j1) * 8 : (u * 8 + j1) * 8 + 8, :] = s
        off_y = by_sublane(PARENT_OFF, lane)
        k_y = corner_yf + off_y
        part_y, line_y = sq_y * (k_y * k_y), y * off_y
        for m in range(4):
            off_x = jnp.where(high, PARENT_OFF[2 * m + 1], PARENT_OFF[2 * m])
            k_x = corner_xf + off_x
            c, s = cos_sin(root(sq_x * (k_x * k_x) + part_y) + (x * off_x + line_y))
            wave[box, 0, 128 + m * 8 : 136 + m * 8, :] = c
            wave[box, 1, 128 + m * 8 : 136 + m * 8, :] = s

        for part in range(4):
            rows = slice(part * 64, part * 64 + 64)
            w_re, w_im = w_ref[0, box, rows, :], w_ref[1, box, rows, :]
            t_re, t_im = turn_c[0, rows, :], turn_c[1, rows, :]
            w_turned[box, 0, rows, :] = w_re * t_re - w_im * t_im
            w_turned[box, 1, rows, :] = w_re * t_im + w_im * t_re

        for e in range(4):
            e1, e2 = e // 2, e % 2
            pick = (2 * (lane // 32) + e1) * 8 + 2 * (lane % 4) + e2
            high_parts = [[], [], [], []]
            low_parts = [[], [], [], []]
            for u in range(2):
                for v in range(2):
                    idx = pick + v * 64
                    for g in range(4):
                        base = (u * 8 + 2 * g) * 8
                        c = jnp.concatenate(
                            [lanes_of(wave[box, 0, base + 8 * i : base + 8 * i + 8, :], idx) for i in (0, 1)]
                        )
                        s = jnp.concatenate(
                            [lanes_of(wave[box, 1, base + 8 * i : base + 8 * i + 8, :], idx) for i in (0, 1)]
                        )
                        at = (u * 2 + v) * 64 + g * 16
                        rows = slice(at, at + 16)
                        for half in range(2):
                            w_re = w_turned[box, 0, rows, half * 128 : half * 128 + 128]
                            w_im = w_turned[box, 1, rows, half * 128 : half * 128 + 128]
                            for z, value in (
                                (half, w_re * c + w_im * s),
                                (2 + half, w_im * c - w_re * s),
                            ):
                                hi, lo = split(value)
                                high_parts[z].append(hi)
                                low_parts[z].append(lo)
            mod_hi = jnp.concatenate([jnp.concatenate(p, axis=0) for p in high_parts], axis=1)
            mod_lo = jnp.concatenate([jnp.concatenate(p, axis=0) for p in low_parts], axis=1)
            first = jnp.dot(tab_ref[...], mod_hi, preferred_element_type=F32)
            second = jnp.dot(tab_ref[0:64, :], mod_lo, preferred_element_type=F32)
            interp = first[0:64] + (first[64:128] + second)
            c = jnp.concatenate(
                [
                    lanes_of(wave[box, 0, 128 + (t // 2) * 8 : 136 + (t // 2) * 8, :], pick + (t % 2) * 64)
                    for t in range(8)
                ]
            )
            s = jnp.concatenate(
                [
                    lanes_of(wave[box, 1, 128 + (t // 2) * 8 : 136 + (t // 2) * 8, :], pick + (t % 2) * 64)
                    for t in range(8)
                ]
            )
            for half in range(2):
                i_re = interp[:, half * 128 : half * 128 + 128]
                i_im = interp[:, half * 128 + 256 : half * 128 + 384]
                t_re = turn_p[0, :, half * 128 : half * 128 + 128]
                t_im = turn_p[1, :, half * 128 : half * 128 + 128]
                g_re = i_re * t_re - i_im * t_im
                g_im = i_re * t_im + i_im * t_re
                out_ref[box, e * 2 + half, 0:64, :] = g_re * c - g_im * s
                out_ref[box, e * 2 + half, 64:128, :] = g_re * s + g_im * c


def source_stage(pos, weights, owner_slot, ranks):
    table = interp_matrix()
    hi = table.astype(jnp.bfloat16)
    lo = (table - hi.astype(np.float32)).astype(jnp.bfloat16)
    stacked = jnp.asarray(np.concatenate([hi, lo], axis=0))
    child = np.array(CHILD_OFF)
    row = np.arange(256)
    off_x = child[row // 128, (row // 8) % 8]
    off_y = child[(row // 64) % 2, row % 8]
    parent = np.array(PARENT_OFF)
    turn_c = jnp.asarray(class_turns(off_x, off_y, -1.0))
    turn_p = jnp.asarray(class_turns(parent[row[:64] // 8], parent[row[:64] % 8], 1.0))

    def whole(*shape):
        return pl.BlockSpec(shape, lambda g, p: (0,) * len(shape))

    return pl.pallas_call(
        source_kernel,
        out_shape=[
            jax.ShapeDtypeStruct((8, 8, 128, 128), F32),
            *[jax.ShapeDtypeStruct((8, 128), I32)] * 5,
        ],
        grid_spec=pltpu.PrefetchScalarGridSpec(
            num_scalar_prefetch=1,
            grid=(4,),
            in_specs=[
                pl.BlockSpec((2, 2, 256, 256), lambda g, p: (0, g, 0, 0)),
                whole(8, 128),
                whole(8, 128),
                whole(128, 256),
                whole(2, 256, 256),
                whole(2, 64, 256),
            ],
            out_specs=[pl.BlockSpec((2, 8, 128, 128), lambda g, p: (g, 0, 0, 0)), *[whole(8, 128)] * 5],
            scratch_shapes=[
                pltpu.VMEM((2, 2, 256, 256), F32),
                pltpu.VMEM((2, 2, 160, 128), F32),
                pltpu.VMEM((16, 1024), BF16),
            ],
        ),
        name="source_stage",
    )(pos, weights, owner_slot, ranks, stacked, turn_c, turn_p)


UNROLL = 16
GROUP = 12
PAIR = 2
MOST_TILES = 96


def target_kernel(
    pos_ref, excl_ref, rank_ref, slot_tile, slot_off, delta_hbm, piv_ref, excl_v, rank_v, out_ref,
    delta, pivots, points_x, points_y, edges, sums, box_of, rows_x, parts, lines, tiles, run, place_of, sem,
):
    def fetch(j, b):
        return pltpu.make_async_copy(
            delta_hbm.at[2 * (b % 4) + b // 4, j], delta.at[j, :, b, :], sem.at[j, b]
        )

    for j in range(8):
        for b in range(8):
            fetch(j, b).start()
    pos = pos_ref[0]
    lane = lax.broadcasted_iota(I32, (8, 128), 1)
    sub = lax.broadcasted_iota(I32, (8, 128), 0)
    sub32 = lax.broadcasted_iota(I32, (32, 128), 0).astype(F32)
    corner_x = 64 * (pos >> 2) - 1024
    turn_x = corner_x.astype(F32) * (1.0 / 2048)
    corner_y = (64 * ((pos & 3) * 8 + 2 * (sub & 3) + (sub >> 2)) - 1024).astype(F32)
    turn_y = corner_y * (1.0 / 2048)
    off_col = by_sublane(PARENT_OFF, lane)
    k_x = corner_x.astype(F32) + off_col
    k_sq_x = k_x * k_x

    for h in range(2):
        p = jnp.transpose(piv_ref[:, h, :].astype(F32))
        for g in range(4):
            pivots[h * 4 + g] = p[g * 32 : g * 32 + 32]
    lane32 = lax.broadcasted_iota(I32, (32, 128), 1)

    def one_block(j, first_tile):
        e1, e2, half = j >> 2, (j >> 1) & 1, j & 1
        pick = half * 64 + 16 * (lane32 >> 5) + 8 * e1 + ((lane32 & 31) >> 2)
        p = lanes_of(pivots[e2], pick)
        for g in range(1, 4):
            other = lanes_of(pivots[(g >> 1) * 4 + 2 * (g & 1) + e2], pick)
            p = jnp.where((lane32 & 3) == g, other, p)
        p = p.astype(I32)
        box_x = 2 * (half * 4 + (lane32 >> 5)) + e1
        box_y = 2 * (lane32 & 31) + e2
        points_x[j] = (32 * box_x + (p >> 5)).astype(F32)
        points_y[j] = (32 * box_y + (p & 31)).astype(F32)
        start_row = jnp.broadcast_to(excl_v[pl.ds(j, 1), :], (8, 128)).astype(F32)
        end_row = start_row + jnp.broadcast_to(rank_v[pl.ds(j, 1), :], (8, 128)).astype(F32)
        edges[j, 0:8, :] = lanes_of(end_row, 8 * sub + 7)
        edges[j, 8:16, :] = lanes_of(end_row, 64 + 8 * sub + 7)
        edges[j, 16:24, :] = lanes_of(end_row, jnp.minimum(8 * lane + sub, 127))
        edges[j, 24:32, :] = start_row
        n_tiles = (excl_ref[j, 127] + rank_ref[j, 127] + 127) >> 7

        def note(k, _):
            run[first_tile + k] = j
            place_of[first_tile + k] = k * 128
            return 0

        lax.fori_loop(0, n_tiles, note, 0)
        return first_tile + n_tiles

    n_all = lax.fori_loop(0, 8, one_block, 0)

    def one_tile(tile):
        j = run[tile]
        row = (place_of[tile] + lane).astype(F32)
        ahead = jnp.where(edges[j, 0:8, :] <= row, 1.0, 0.0)
        ahead = ahead + jnp.where(edges[j, 8:16, :] <= row, 1.0, 0.0)
        group = jnp.minimum(jnp.sum(ahead, axis=0, keepdims=True), 15.0)
        group = jnp.broadcast_to(group, (8, 128))
        inner = jnp.where(lanes_of(edges[j, 16:24, :], group.astype(I32)) <= row, 1.0, 0.0)
        inner = jnp.broadcast_to(jnp.sum(inner, axis=0, keepdims=True), (8, 128))
        idx = jnp.minimum(8.0 * group + inner, 127.0).astype(I32)
        place = row - lanes_of(edges[j, 24:32, :], idx)
        idx32 = jnp.concatenate([idx] * 4)
        mine = sub32 == jnp.concatenate([place] * 4)
        got_x = jnp.where(mine, lanes_of(points_x[j], idx32), 0.0)
        got_y = jnp.where(mine, lanes_of(points_y[j], idx32), 0.0)
        h_x = jnp.broadcast_to(jnp.sum(got_x, axis=0, keepdims=True), (8, 128))
        h_y = jnp.broadcast_to(jnp.sum(got_y, axis=0, keepdims=True), (8, 128))
        sq_x, sq_y = speeds(h_x * (1.0 / 256), h_y * (1.0 / 256))
        x, y = h_x * (1.0 / 2048), h_y * (1.0 / 2048)
        whole_y = wrap(h_y * turn_y)
        part, line = [], []
        for off in PARENT_OFF:
            k_y = corner_y + off
            part.append(sq_y * (k_y * k_y))
            line.append(wrap(whole_y + y * off))
        return idx, sq_x * k_sq_x, wrap(h_x * turn_x) + x * off_col, part, line

    def one_group(i, _):
        at = [jnp.minimum(i * GROUP + h, n_all - 1) for h in range(GROUP)]
        found = [one_tile(tile) for tile in at]
        for tile, (idx, part_x, line_x, part, line) in zip(at, found):
            box_of[tile] = idx
            rows_x[tile, 0:8, :] = part_x
            rows_x[tile, 8:16, :] = line_x
            for t2 in range(8):
                parts[tile, t2] = part[t2]
                lines[tile, t2] = line[t2]
        return 0

    lax.fori_loop(0, (n_all + GROUP - 1) // GROUP, one_group, 0)

    def one_total(j, _):
        for b in range(8):
            fetch(j, b).wait()
        total_re = jnp.zeros((8, 128), F32)
        total_im = jnp.zeros((8, 128), F32)
        for t in range(64):
            total_re = total_re + delta[j, t]
            total_im = total_im + delta[j, 64 + t]
        sums[j, 0:8, :] = total_re
        sums[j, 8:16, :] = total_im
        return 0

    lax.fori_loop(0, 8, one_total, 0)

    def one_sum(tile):
        j = run[tile]
        idx = box_of[tile]
        acc_re = lanes_of(sums[j, 0:8, :], idx)
        acc_im = lanes_of(sums[j, 8:16, :], idx)
        for t1 in range(8):
            part_x = jnp.broadcast_to(rows_x[tile, t1 : t1 + 1, :], (8, 128))
            line_x = jnp.broadcast_to(rows_x[tile, 8 + t1 : 9 + t1, :], (8, 128))
            for t2 in range(8):
                t = t1 * 8 + t2
                d_re = lanes_of(delta[j, t], idx)
                d_im = lanes_of(delta[j, 64 + t], idx)
                d, s = sine_parts(
                    root(part_x + parts[tile, t2]) + (line_x + lines[tile, t2]), SIN_C
                )
                acc_re = acc_re - (d * d_re + s * d_im)
                acc_im = acc_im + (s * d_re - d * d_im)
        acc_re = acc_re + pltpu.roll(acc_re, 4, 0)
        acc_im = acc_im + pltpu.roll(acc_im, 4, 0)
        return jnp.where(sub < 4, acc_re, acc_im)

    def one_pair(i, _):
        at = [jnp.minimum(i * PAIR + h, n_all - 1) for h in range(PAIR)]
        done = [one_sum(tile) for tile in at]
        for tile, value in zip(at, done):
            tiles[tile] = value
        return 0

    lax.fori_loop(0, (n_all + PAIR - 1) // PAIR, one_pair, 0)

    def one_owner(o, _):
        for part in range(2):
            out = jnp.zeros((8, 128), F32)
            for q in range(4):
                tile = slot_tile[o * 8 + part * 4 + q]
                off = slot_off[o * 8 + part * 4 + q]
                joined = jnp.where(lane >= off, tiles[tile], tiles[tile + 1])
                joined = pltpu.roll(joined, (q * 32 + 128 - off) & 127, 1)
                out = joined if q == 0 else jnp.where((lane >> 5) == q, joined, out)
            out_ref[o, :, part * 128 : part * 128 + 128] = out
        return 0

    lax.fori_loop(0, 128, one_owner, 0, unroll=UNROLL)


def target_stage(pos, excl, rank, slot_tile, slot_off, delta, piv):
    smem = pl.BlockSpec(memory_space=pltpu.SMEM)
    vmem = pl.BlockSpec(memory_space=pltpu.VMEM)
    hbm = pl.BlockSpec(memory_space=pl.ANY)
    return pl.pallas_call(
        target_kernel,
        out_shape=jax.ShapeDtypeStruct((128, 8, 256), F32),
        in_specs=[smem, smem, smem, smem, smem, hbm, vmem, vmem, vmem],
        out_specs=vmem,
        scratch_shapes=[
            pltpu.VMEM((8, 128, 8, 128), F32),
            pltpu.VMEM((8, 32, 128), F32),
            pltpu.VMEM((8, 32, 128), F32),
            pltpu.VMEM((8, 32, 128), F32),
            pltpu.VMEM((8, 32, 128), F32),
            pltpu.VMEM((8, 16, 128), F32),
            pltpu.VMEM((MOST_TILES, 8, 128), I32),
            pltpu.VMEM((MOST_TILES, 16, 128), F32),
            pltpu.VMEM((MOST_TILES, 8, 8, 128), F32),
            pltpu.VMEM((MOST_TILES, 8, 8, 128), F32),
            pltpu.VMEM((MOST_TILES, 8, 128), F32),
            pltpu.SMEM((MOST_TILES,), I32),
            pltpu.SMEM((MOST_TILES,), I32),
            pltpu.SemaphoreType.DMA((8, 8)),
        ],
        name="target_stage",
    )(
        pos, excl, rank, slot_tile.reshape(1024), slot_off.reshape(1024), delta, piv, excl, rank
    )


def owner_kernel(pos_ref, rank_ref, in_ref, out_ref, gathered):
    pos = pos_ref[0]
    sub = lax.broadcasted_iota(I32, (8, 256), 0)
    for p1 in range(16):
        part = [in_ref[p1 * 8 + q] + in_ref[p1 * 8 + 4 + q] for q in range(4)]
        for m in range(2):
            even, odd = part[2 * m], part[2 * m + 1]
            row = p1 * 16 + m * 8
            gathered[0, row : row + 8, :] = jnp.where(sub < 4, even, pltpu.roll(odd, 4, 0))
            gathered[1, row : row + 8, :] = jnp.where(sub < 4, pltpu.roll(even, 4, 0), odd)
    i = lax.broadcasted_iota(I32, (32, 256), 0)
    for z in range(2):
        rows = jnp.transpose(gathered[z])
        for k in range(8):
            live = i < rank_ref[pos >> 4, (pos & 15) * 8 + k]
            out_ref[z, :, k, :] = jnp.where(live, rows[k * 32 : k * 32 + 32], 0.0)


def owner_stage(pos, rank, received):
    smem = pl.BlockSpec(memory_space=pltpu.SMEM)
    vmem = pl.BlockSpec(memory_space=pltpu.VMEM)
    return pl.pallas_call(
        owner_kernel,
        out_shape=jax.ShapeDtypeStruct((2, 32, 8, 256), F32),
        in_specs=[smem, smem, vmem],
        out_specs=vmem,
        scratch_shapes=[pltpu.VMEM((2, 256, 256), F32)],
        name="owner_stage",
    )(pos, rank, received)


def local(child_weights, pivots, ranks, owner_slot):
    pos = lax.axis_index("grp") * lax.axis_size("dev") + lax.axis_index("dev")
    pos = pos.astype(I32).reshape(1)
    spread = jnp.broadcast_to(pivots.reshape(1, 2, 128), (128, 2, 128))
    all_pivots = lax.all_to_all(spread, AXES, split_axis=0, concat_axis=0, tiled=True)
    at = owner_slot.reshape(8, 128)
    weights = child_weights.reshape(2, 8, 256, 256)
    delta, excl, rank, slot_tile, slot_off, slot_rank = source_stage(
        pos, weights, at, ranks.reshape(8, 128)
    )
    send = target_stage(pos, excl, rank, slot_tile, slot_off, delta, all_pivots)
    received = lax.all_to_all(send, AXES, split_axis=0, concat_axis=0, tiled=True)
    return owner_stage(pos, slot_rank, received)


def solution(mesh):
    in_specs = (P(None, AXES, None, None, None), P(AXES, None), P(), P())
    out_specs = P(None, None, AXES, None)
    return jax.shard_map(local, mesh=mesh, in_specs=in_specs, out_specs=out_specs, check_vma=False)
```

```python
import numpy as np

import jax
import jax.numpy as jnp
from jax import lax
from jax.experimental import pallas as pl
from jax.experimental.pallas import tpu as pltpu
from jax.sharding import PartitionSpec as P

AXES = ("grp", "dev")
F32 = jnp.float32
BF16 = jnp.bfloat16
I32 = jnp.int32

SIN_C = (2.6417391300201416, -1.0859273672103882, 0.13053695857524872)
SIN_FINE = (2.641753911972046, -1.0863757133483887, 0.1339970976114273, -0.007720405701547861)
ROOT2 = 1.4142135623730951
ROOT8 = 2.8284271247461903


def _f32(x):
    return np.float32(x)


CHEB = [_f32(np.cos(np.pi * (2 * j + 1) / 16.0)) for j in range(8)]
PARENT_OFF = [float(_f32(31.5) + _f32(32.0) * c) for c in CHEB]
CHILD_OFF = [[float(_f32(32.0 * u + 15.5) + _f32(16.0) * c) for c in CHEB] for u in range(2)]


def interp_matrix():
    nodes = np.cos(np.pi * (2 * np.arange(8) + 1) / 16.0)
    halves = np.zeros((2, 8, 8))
    for u in range(2):
        points = u - 0.5 + 0.5 * nodes
        for t in range(8):
            value = np.ones(8)
            for s in range(8):
                if s != t:
                    value = value * (points - nodes[s]) / (nodes[t] - nodes[s])
            halves[u, t] = value
    full = np.einsum("uaj,vbk->abuvjk", halves, halves).reshape(64, 256)
    return full.astype(np.float32)


def class_turns(off_x, off_y, sign):
    lane = np.arange(256)
    a, b = lane // 128, (lane % 32) // 4
    cycles = (np.outer(off_x, a) + np.outer(off_y, b)) / 8.0
    angle = sign * 2.0 * np.pi * (cycles % 1.0)
    return np.stack([np.cos(angle), np.sin(angle)]).astype(np.float32)


def wrap(x):
    return x - jnp.round(x)


def sine_parts(phase, coef):
    r = wrap(phase)
    z = r * r
    s = coef[-1]
    for c in coef[-2::-1]:
        s = s * z + c
    s = s * r
    q = s * s
    w = ROOT8 - q
    v = w * lax.rsqrt(w)
    return q * w, (s * v) * (ROOT2 - q)


def cos_sin(phase, coef=SIN_C):
    d, s = sine_parts(phase, coef)
    return 1.0 - d, s


def root(x):
    return x * lax.rsqrt(x)


def speeds(turn_x, turn_y):
    sub = lax.broadcasted_iota(I32, turn_x.shape, 0)
    c, s = cos_sin(jnp.where(sub < 4, turn_x, turn_y), SIN_FINE)
    c1 = (2.0 + s * pltpu.roll(s, 4, 0)) * 0.0625
    c2 = (2.0 + c * pltpu.roll(c, 4, 0)) * 0.0625
    return c1 * c1, c2 * c2


def split(x):
    hi = x.astype(BF16)
    return hi, (x - hi.astype(F32)).astype(BF16)


def by_sublane(values, like):
    sub = lax.broadcasted_iota(I32, like.shape, 0)
    out = jnp.full(like.shape, values[0], F32)
    for s in range(1, 8):
        out = jnp.where(sub == s, values[s], out)
    return out


def lanes_of(x, idx):
    return jnp.take_along_axis(x, idx, axis=1)


NT = (((1,), (1,)), ((), ()))


def source_kernel(
    pos_ref, w_ref, os_ref, ranks_ref, tab_ref, turn_c, turn_p,
    out_ref, excl_ref, rank_ref, slot_tile_ref, slot_off_ref, slot_rank_ref, tile_ref,
    w_turned, wave, labels,
):
    step = pl.program_id(0)
    pos = pos_ref[0]
    lane = lax.broadcasted_iota(I32, (8, 128), 1)
    sub = lax.broadcasted_iota(I32, (8, 128), 0)

    @pl.when(step == 0)
    def _():
        ranks = ranks_ref[...].astype(F32)
        owners = os_ref[...].astype(F32)
        rank8 = jnp.zeros((8, 128), F32)
        at_row = []
        for n in range(8):
            e1, e2, half = n // 4, (n // 2) % 2, n % 2
            idx = e1 * 64 + 2 * (lane % 32) + e2
            mine = sub == 4 * half + lane // 32
            at_row.append(
                jnp.sum(jnp.where(mine, lanes_of(owners, idx), 0.0), axis=0, keepdims=True)
            )
            rk = jnp.sum(jnp.where(mine, lanes_of(ranks, idx), 0.0), axis=0, keepdims=True)
            rank8 = jnp.where(sub == n, jnp.broadcast_to(rk, (8, 128)), rank8)
        upto = (
            lax.broadcasted_iota(I32, (128, 128), 0) <= lax.broadcasted_iota(I32, (128, 128), 1)
        )
        upto = jnp.where(upto, 1.0, 0.0).astype(BF16)
        excl8 = jnp.dot(rank8.astype(BF16), upto, preferred_element_type=F32) - rank8
        rank_ref[...] = rank8.astype(I32)
        excl_ref[...] = excl8.astype(I32)
        live = lanes_of(excl8 + rank8, jnp.full((8, 128), 127, I32)).astype(I32)
        n_tiles = (live + 127) >> 7
        first = jnp.zeros((1, 128), I32)
        tile = lane[0:1]
        tile_box, tile_first = jnp.zeros((1, 128), I32), jnp.zeros((1, 128), I32)
        row = lax.broadcasted_iota(I32, (16, 128), 0)
        for n in range(8):
            rk = jnp.broadcast_to(rank8[n : n + 1], (16, 128))
            ahead = jnp.broadcast_to(excl8[n : n + 1], (16, 128)).astype(I32)
            high, low = (ahead >> 6).astype(F32), (ahead & 63).astype(F32)
            label = jnp.where(row == 2, high, jnp.where(row == 3, low, 0.0))
            start = jnp.broadcast_to(first.astype(F32), (16, 128))
            label = jnp.where(row == 0, rk, jnp.where(row == 1, start, label))
            tile_box = jnp.where(tile >= first, n, tile_box)
            tile_first = jnp.where(tile >= first, first, tile_first)
            first = first + n_tiles[n : n + 1]
            labels[:, n * 128 : n * 128 + 128] = label.astype(BF16)
        tile_ref[0:1, :] = tile_box
        tile_ref[1:2, :] = (tile - tile_first) * 128
        tile_ref[2:3, :] = first
        tile_ref[3:8, :] = jnp.zeros((5, 128), I32)
        for j in range(8):
            slot = lax.broadcasted_iota(I32, (128, 128), 0).astype(F32) + j * 128.0
            got = jnp.zeros((16, 128), F32)
            for n in range(8):
                hit = jnp.where(slot == jnp.broadcast_to(at_row[n], (128, 128)), 1.0, 0.0)
                got = got + lax.dot_general(
                    labels[:, n * 128 : n * 128 + 128], hit.astype(BF16), NT,
                    preferred_element_type=F32,
                )
            slot_rank_ref[j : j + 1, :] = got[0:1].astype(I32)
            at = (got[1:2] * 128.0 + got[2:3] * 64.0 + got[3:4]).astype(I32)
            slot_tile_ref[j : j + 1, :] = at >> 7
            slot_off_ref[j : j + 1, :] = at & 127

    corner_xf = (64 * (pos // 4) - 1024).astype(F32)
    h_x = 64 * ((lane % 64) // 8) + 31
    h_y = 64 * (lane % 8) + 31
    h_xf, h_yf = h_x.astype(F32), h_y.astype(F32)
    sq_x, sq_y = speeds(h_xf * (1.0 / 512), h_yf * (1.0 / 512))
    x, y = h_xf * (1.0 / 4096), h_yf * (1.0 / 4096)
    high = lane >= 64

    for box in range(2):
        corner_yf = (64 * ((pos % 4) * 8 + 2 * step + box) - 1024).astype(F32)
        off_y = jnp.where(high, by_sublane(CHILD_OFF[1], lane), by_sublane(CHILD_OFF[0], lane))
        k_y = corner_yf + off_y
        part_y, line_y = sq_y * (k_y * k_y), y * off_y
        for u in range(2):
            for j1 in range(8):
                off_x = CHILD_OFF[u][j1]
                k_x = corner_xf + off_x
                c, s = cos_sin(root(sq_x * (k_x * k_x) + part_y) + (x * off_x + line_y))
                wave[box, 0, (u * 8 + j1) * 8 : (u * 8 + j1) * 8 + 8, :] = c
                wave[box, 1, (u * 8 + j1) * 8 : (u * 8 + j1) * 8 + 8, :] = s
        off_y = by_sublane(PARENT_OFF, lane)
        k_y = corner_yf + off_y
        part_y, line_y = sq_y * (k_y * k_y), y * off_y
        for m in range(4):
            off_x = jnp.where(high, PARENT_OFF[2 * m + 1], PARENT_OFF[2 * m])
            k_x = corner_xf + off_x
            c, s = cos_sin(root(sq_x * (k_x * k_x) + part_y) + (x * off_x + line_y))
            wave[box, 0, 128 + m * 8 : 136 + m * 8, :] = c
            wave[box, 1, 128 + m * 8 : 136 + m * 8, :] = s

        for part in range(4):
            rows = slice(part * 64, part * 64 + 64)
            w_re, w_im = w_ref[0, box, rows, :], w_ref[1, box, rows, :]
            t_re, t_im = turn_c[0, rows, :], turn_c[1, rows, :]
            w_turned[box, 0, rows, :] = w_re * t_re - w_im * t_im
            w_turned[box, 1, rows, :] = w_re * t_im + w_im * t_re

        for e in range(4):
            e1, e2 = e // 2, e % 2
            pick = (2 * (lane // 32) + e1) * 8 + 2 * (lane % 4) + e2
            high_parts = [[], [], [], []]
            low_parts = [[], [], [], []]
            for u in range(2):
                for v in range(2):
                    idx = pick + v * 64
                    for g in range(4):
                        base = (u * 8 + 2 * g) * 8
                        c = jnp.concatenate(
                            [lanes_of(wave[box, 0, base + 8 * i : base + 8 * i + 8, :], idx) for i in (0, 1)]
                        )
                        s = jnp.concatenate(
                            [lanes_of(wave[box, 1, base + 8 * i : base + 8 * i + 8, :], idx) for i in (0, 1)]
                        )
                        at = (u * 2 + v) * 64 + g * 16
                        rows = slice(at, at + 16)
                        for half in range(2):
                            w_re = w_turned[box, 0, rows, half * 128 : half * 128 + 128]
                            w_im = w_turned[box, 1, rows, half * 128 : half * 128 + 128]
                            for z, value in (
                                (half, w_re * c + w_im * s),
                                (2 + half, w_im * c - w_re * s),
                            ):
                                hi, lo = split(value)
                                high_parts[z].append(hi)
                                low_parts[z].append(lo)
            mod_hi = jnp.concatenate([jnp.concatenate(p, axis=0) for p in high_parts], axis=1)
            mod_lo = jnp.concatenate([jnp.concatenate(p, axis=0) for p in low_parts], axis=1)
            first = jnp.dot(tab_ref[...], mod_hi, preferred_element_type=F32)
            second = jnp.dot(tab_ref[0:64, :], mod_lo, preferred_element_type=F32)
            interp = first[0:64] + (first[64:128] + second)
            c = jnp.concatenate(
                [
                    lanes_of(wave[box, 0, 128 + (t // 2) * 8 : 136 + (t // 2) * 8, :], pick + (t % 2) * 64)
                    for t in range(8)
                ]
            )
            s = jnp.concatenate(
                [
                    lanes_of(wave[box, 1, 128 + (t // 2) * 8 : 136 + (t // 2) * 8, :], pick + (t % 2) * 64)
                    for t in range(8)
                ]
            )
            for half in range(2):
                i_re = interp[:, half * 128 : half * 128 + 128]
                i_im = interp[:, half * 128 + 256 : half * 128 + 384]
                t_re = turn_p[0, :, half * 128 : half * 128 + 128]
                t_im = turn_p[1, :, half * 128 : half * 128 + 128]
                g_re = i_re * t_re - i_im * t_im
                g_im = i_re * t_im + i_im * t_re
                out_ref[box, e * 2 + half, 0:64, :] = g_re * c - g_im * s
                out_ref[box, e * 2 + half, 64:128, :] = g_re * s + g_im * c


def source_stage(pos, weights, owner_slot, ranks):
    table = interp_matrix()
    hi = table.astype(jnp.bfloat16)
    lo = (table - hi.astype(np.float32)).astype(jnp.bfloat16)
    stacked = jnp.asarray(np.concatenate([hi, lo], axis=0))
    child = np.array(CHILD_OFF)
    row = np.arange(256)
    off_x = child[row // 128, (row // 8) % 8]
    off_y = child[(row // 64) % 2, row % 8]
    parent = np.array(PARENT_OFF)
    turn_c = jnp.asarray(class_turns(off_x, off_y, -1.0))
    turn_p = jnp.asarray(class_turns(parent[row[:64] // 8], parent[row[:64] % 8], 1.0))

    def whole(*shape):
        return pl.BlockSpec(shape, lambda g, p: (0,) * len(shape))

    return pl.pallas_call(
        source_kernel,
        out_shape=[
            jax.ShapeDtypeStruct((8, 8, 128, 128), F32),
            *[jax.ShapeDtypeStruct((8, 128), I32)] * 6,
        ],
        grid_spec=pltpu.PrefetchScalarGridSpec(
            num_scalar_prefetch=1,
            grid=(4,),
            in_specs=[
                pl.BlockSpec((2, 2, 256, 256), lambda g, p: (0, g, 0, 0)),
                whole(8, 128),
                whole(8, 128),
                whole(128, 256),
                whole(2, 256, 256),
                whole(2, 64, 256),
            ],
            out_specs=[pl.BlockSpec((2, 8, 128, 128), lambda g, p: (g, 0, 0, 0)), *[whole(8, 128)] * 6],
            scratch_shapes=[
                pltpu.VMEM((2, 2, 256, 256), F32),
                pltpu.VMEM((2, 2, 160, 128), F32),
                pltpu.VMEM((16, 1024), BF16),
            ],
        ),
        name="source_stage",
    )(pos, weights, owner_slot, ranks, stacked, turn_c, turn_p)


UNROLL = 16
GROUP = 12
PAIR = 2
MOST_TILES = 96


def target_kernel(
    pos_ref, tile_at, slot_tile, slot_off, delta_hbm, piv_ref, excl_v, rank_v, out_ref,
    delta, pivots, points_x, points_y, edges, sums, box_of, rows_x, parts, lines, tiles, sem,
):
    def fetch(j, b):
        return pltpu.make_async_copy(
            delta_hbm.at[2 * (b % 4) + b // 4, j], delta.at[j, :, b, :], sem.at[j, b]
        )

    for j in range(8):
        for b in range(8):
            fetch(j, b).start()
    pos = pos_ref[0]
    lane = lax.broadcasted_iota(I32, (8, 128), 1)
    sub = lax.broadcasted_iota(I32, (8, 128), 0)
    sub32 = lax.broadcasted_iota(I32, (32, 128), 0).astype(F32)
    corner_x = 64 * (pos >> 2) - 1024
    turn_x = corner_x.astype(F32) * (1.0 / 2048)
    corner_y = (64 * ((pos & 3) * 8 + 2 * (sub & 3) + (sub >> 2)) - 1024).astype(F32)
    turn_y = corner_y * (1.0 / 2048)
    off_col = by_sublane(PARENT_OFF, lane)
    k_x = corner_x.astype(F32) + off_col
    k_sq_x = k_x * k_x

    for h in range(2):
        p = jnp.transpose(piv_ref[:, h, :].astype(F32))
        for g in range(4):
            pivots[h * 4 + g] = p[g * 32 : g * 32 + 32]
    lane32 = lax.broadcasted_iota(I32, (32, 128), 1)

    for j in range(8):
        e1, e2, half = j // 4, (j // 2) % 2, j % 2
        pick = half * 64 + 16 * (lane32 >> 5) + 8 * e1 + ((lane32 & 31) >> 2)
        p = lanes_of(pivots[e2], pick)
        for g in range(1, 4):
            other = lanes_of(pivots[(g >> 1) * 4 + 2 * (g & 1) + e2], pick)
            p = jnp.where((lane32 & 3) == g, other, p)
        p = p.astype(I32)
        box_x = 2 * (half * 4 + (lane32 >> 5)) + e1
        box_y = 2 * (lane32 & 31) + e2
        points_x[j] = (32 * box_x + (p >> 5)).astype(F32)
        points_y[j] = (32 * box_y + (p & 31)).astype(F32)
        start_row = jnp.broadcast_to(excl_v[j : j + 1, :], (8, 128)).astype(F32)
        end_row = start_row + jnp.broadcast_to(rank_v[j : j + 1, :], (8, 128)).astype(F32)
        edges[j, 0:8, :] = lanes_of(end_row, 8 * sub + 7)
        edges[j, 8:16, :] = lanes_of(end_row, 64 + 8 * sub + 7)
        edges[j, 16:24, :] = lanes_of(end_row, jnp.minimum(8 * lane + sub, 127))
        edges[j, 24:32, :] = start_row
    n_all = tile_at[2, 0]

    def one_tile(tile):
        j = tile_at[0, tile]
        row = (tile_at[1, tile] + lane).astype(F32)
        ahead = jnp.where(edges[j, 0:8, :] <= row, 1.0, 0.0)
        ahead = ahead + jnp.where(edges[j, 8:16, :] <= row, 1.0, 0.0)
        group = jnp.minimum(jnp.sum(ahead, axis=0, keepdims=True), 15.0)
        group = jnp.broadcast_to(group, (8, 128))
        inner = jnp.where(lanes_of(edges[j, 16:24, :], group.astype(I32)) <= row, 1.0, 0.0)
        inner = jnp.broadcast_to(jnp.sum(inner, axis=0, keepdims=True), (8, 128))
        idx = jnp.minimum(8.0 * group + inner, 127.0).astype(I32)
        place = row - lanes_of(edges[j, 24:32, :], idx)
        idx32 = jnp.concatenate([idx] * 4)
        mine = sub32 == jnp.concatenate([place] * 4)
        got_x = jnp.where(mine, lanes_of(points_x[j], idx32), 0.0)
        got_y = jnp.where(mine, lanes_of(points_y[j], idx32), 0.0)
        h_x = jnp.broadcast_to(jnp.sum(got_x, axis=0, keepdims=True), (8, 128))
        h_y = jnp.broadcast_to(jnp.sum(got_y, axis=0, keepdims=True), (8, 128))
        sq_x, sq_y = speeds(h_x * (1.0 / 256), h_y * (1.0 / 256))
        x, y = h_x * (1.0 / 2048), h_y * (1.0 / 2048)
        whole_y = wrap(h_y * turn_y)
        part, line = [], []
        for off in PARENT_OFF:
            k_y = corner_y + off
            part.append(sq_y * (k_y * k_y))
            line.append(wrap(whole_y + y * off))
        return idx, sq_x * k_sq_x, wrap(h_x * turn_x) + x * off_col, part, line

    def one_group(i, _):
        at = [jnp.minimum(i * GROUP + h, n_all - 1) for h in range(GROUP)]
        found = [one_tile(tile) for tile in at]
        for tile, (idx, part_x, line_x, part, line) in zip(at, found):
            box_of[tile] = idx
            rows_x[tile, 0:8, :] = part_x
            rows_x[tile, 8:16, :] = line_x
            for t2 in range(8):
                parts[tile, t2] = part[t2]
                lines[tile, t2] = line[t2]
        return 0

    lax.fori_loop(0, (n_all + GROUP - 1) // GROUP, one_group, 0)

    def one_total(j, _):
        for b in range(8):
            fetch(j, b).wait()
        total_re = jnp.zeros((8, 128), F32)
        total_im = jnp.zeros((8, 128), F32)
        for t in range(64):
            total_re = total_re + delta[j, t]
            total_im = total_im + delta[j, 64 + t]
        sums[j, 0:8, :] = total_re
        sums[j, 8:16, :] = total_im
        return 0

    lax.fori_loop(0, 8, one_total, 0)

    def one_sum(tile):
        j = tile_at[0, tile]
        idx = box_of[tile]
        acc_re = lanes_of(sums[j, 0:8, :], idx)
        acc_im = lanes_of(sums[j, 8:16, :], idx)
        for t1 in range(8):
            part_x = jnp.broadcast_to(rows_x[tile, t1 : t1 + 1, :], (8, 128))
            line_x = jnp.broadcast_to(rows_x[tile, 8 + t1 : 9 + t1, :], (8, 128))
            for t2 in range(8):
                t = t1 * 8 + t2
                d_re = lanes_of(delta[j, t], idx)
                d_im = lanes_of(delta[j, 64 + t], idx)
                d, s = sine_parts(
                    root(part_x + parts[tile, t2]) + (line_x + lines[tile, t2]), SIN_C
                )
                acc_re = acc_re - (d * d_re + s * d_im)
                acc_im = acc_im + (s * d_re - d * d_im)
        acc_re = acc_re + pltpu.roll(acc_re, 4, 0)
        acc_im = acc_im + pltpu.roll(acc_im, 4, 0)
        return jnp.where(sub < 4, acc_re, acc_im)

    def one_pair(i, _):
        at = [jnp.minimum(i * PAIR + h, n_all - 1) for h in range(PAIR)]
        done = [one_sum(tile) for tile in at]
        for tile, value in zip(at, done):
            tiles[tile] = value
        return 0

    lax.fori_loop(0, (n_all + PAIR - 1) // PAIR, one_pair, 0)

    def one_owner(o, _):
        for part in range(2):
            out = jnp.zeros((8, 128), F32)
            for q in range(4):
                tile = slot_tile[o * 8 + part * 4 + q]
                off = slot_off[o * 8 + part * 4 + q]
                joined = jnp.where(lane >= off, tiles[tile], tiles[tile + 1])
                joined = pltpu.roll(joined, (q * 32 + 128 - off) & 127, 1)
                out = joined if q == 0 else jnp.where((lane >> 5) == q, joined, out)
            out_ref[o, :, part * 128 : part * 128 + 128] = out
        return 0

    lax.fori_loop(0, 128, one_owner, 0, unroll=UNROLL)


def target_stage(pos, excl, rank, slot_tile, slot_off, tile_at, delta, piv):
    smem = pl.BlockSpec(memory_space=pltpu.SMEM)
    vmem = pl.BlockSpec(memory_space=pltpu.VMEM)
    hbm = pl.BlockSpec(memory_space=pl.ANY)
    return pl.pallas_call(
        target_kernel,
        out_shape=pltpu.VMEM((128, 8, 256), F32),
        in_specs=[smem, smem, smem, smem, hbm, vmem, vmem, vmem],
        out_specs=vmem,
        scratch_shapes=[
            pltpu.VMEM((8, 128, 8, 128), F32),
            pltpu.VMEM((8, 32, 128), F32),
            pltpu.VMEM((8, 32, 128), F32),
            pltpu.VMEM((8, 32, 128), F32),
            pltpu.VMEM((8, 32, 128), F32),
            pltpu.VMEM((8, 16, 128), F32),
            pltpu.VMEM((MOST_TILES, 8, 128), I32),
            pltpu.VMEM((MOST_TILES, 16, 128), F32),
            pltpu.VMEM((MOST_TILES, 8, 8, 128), F32),
            pltpu.VMEM((MOST_TILES, 8, 8, 128), F32),
            pltpu.VMEM((MOST_TILES, 8, 128), F32),
            pltpu.SemaphoreType.DMA((8, 8)),
        ],
        name="target_stage",
    )(
        pos, tile_at, slot_tile.reshape(1024), slot_off.reshape(1024), delta, piv, excl, rank
    )


def owner_kernel(pos_ref, rank_ref, in_ref, out_ref, gathered):
    pos = pos_ref[0]
    sub = lax.broadcasted_iota(I32, (8, 256), 0)
    for p1 in range(16):
        part = [in_ref[p1 * 8 + q] + in_ref[p1 * 8 + 4 + q] for q in range(4)]
        for m in range(2):
            even, odd = part[2 * m], part[2 * m + 1]
            row = p1 * 16 + m * 8
            gathered[0, row : row + 8, :] = jnp.where(sub < 4, even, pltpu.roll(odd, 4, 0))
            gathered[1, row : row + 8, :] = jnp.where(sub < 4, pltpu.roll(even, 4, 0), odd)
    i = lax.broadcasted_iota(I32, (32, 256), 0)
    for z in range(2):
        rows = jnp.transpose(gathered[z])
        for k in range(8):
            live = i < rank_ref[pos >> 4, (pos & 15) * 8 + k]
            out_ref[z, :, k, :] = jnp.where(live, rows[k * 32 : k * 32 + 32], 0.0)


def owner_stage(pos, rank, received):
    smem = pl.BlockSpec(memory_space=pltpu.SMEM)
    vmem = pl.BlockSpec(memory_space=pltpu.VMEM)
    return pl.pallas_call(
        owner_kernel,
        out_shape=jax.ShapeDtypeStruct((2, 32, 8, 256), F32),
        in_specs=[smem, smem, vmem],
        out_specs=vmem,
        scratch_shapes=[pltpu.VMEM((2, 256, 256), F32)],
        name="owner_stage",
    )(pos, rank, received)


def local(child_weights, pivots, ranks, owner_slot):
    pos = lax.axis_index("grp") * lax.axis_size("dev") + lax.axis_index("dev")
    pos = pos.astype(I32).reshape(1)
    spread = jnp.broadcast_to(pivots.reshape(1, 2, 128), (128, 2, 128))
    all_pivots = lax.all_to_all(spread, AXES, split_axis=0, concat_axis=0, tiled=True)
    at = owner_slot.reshape(8, 128)
    weights = child_weights.reshape(2, 8, 256, 256)
    delta, excl, rank, slot_tile, slot_off, slot_rank, tile_at = source_stage(
        pos, weights, at, ranks.reshape(8, 128)
    )
    all_pivots = pltpu.with_memory_space_constraint(all_pivots, pltpu.VMEM)
    send = target_stage(pos, excl, rank, slot_tile, slot_off, tile_at, delta, all_pivots)
    received = lax.all_to_all(send, AXES, split_axis=0, concat_axis=0, tiled=True)
    received = pltpu.with_memory_space_constraint(received, pltpu.VMEM)
    return owner_stage(pos, slot_rank, received)


def solution(mesh):
    in_specs = (P(None, AXES, None, None, None), P(AXES, None), P(), P())
    out_specs = P(None, None, AXES, None)
    return jax.shard_map(local, mesh=mesh, in_specs=in_specs, out_specs=out_specs, check_vma=False)
```

```python
import numpy as np

import jax
import jax.numpy as jnp
from jax import lax
from jax.experimental import pallas as pl
from jax.experimental.pallas import tpu as pltpu
from jax.sharding import PartitionSpec as P

AXES = ("grp", "dev")
F32 = jnp.float32
BF16 = jnp.bfloat16
I32 = jnp.int32

SIN_C = (2.6417391300201416, -1.0859273672103882, 0.13053695857524872)
SIN_FINE = (2.641753911972046, -1.0863757133483887, 0.1339970976114273, -0.007720405701547861)
ROOT2 = 1.4142135623730951
ROOT8 = 2.8284271247461903


def _f32(x):
    return np.float32(x)


CHEB = [_f32(np.cos(np.pi * (2 * j + 1) / 16.0)) for j in range(8)]
PARENT_OFF = [float(_f32(31.5) + _f32(32.0) * c) for c in CHEB]
CHILD_OFF = [[float(_f32(32.0 * u + 15.5) + _f32(16.0) * c) for c in CHEB] for u in range(2)]


def interp_matrix():
    nodes = np.cos(np.pi * (2 * np.arange(8) + 1) / 16.0)
    halves = np.zeros((2, 8, 8))
    for u in range(2):
        points = u - 0.5 + 0.5 * nodes
        for t in range(8):
            value = np.ones(8)
            for s in range(8):
                if s != t:
                    value = value * (points - nodes[s]) / (nodes[t] - nodes[s])
            halves[u, t] = value
    full = np.einsum("uaj,vbk->abuvjk", halves, halves).reshape(64, 256)
    return full.astype(np.float32)


def class_turns(off_x, off_y, sign):
    lane = np.arange(256)
    a, b = lane // 128, (lane % 32) // 4
    cycles = (np.outer(off_x, a) + np.outer(off_y, b)) / 8.0
    angle = sign * 2.0 * np.pi * (cycles % 1.0)
    return np.stack([np.cos(angle), np.sin(angle)]).astype(np.float32)


def wrap(x):
    return x - jnp.round(x)


def sine_parts(phase, coef):
    r = wrap(phase)
    z = r * r
    s = coef[-1]
    for c in coef[-2::-1]:
        s = s * z + c
    s = s * r
    q = s * s
    w = ROOT8 - q
    v = w * lax.rsqrt(w)
    return q * w, (s * v) * (ROOT2 - q)


def cos_sin(phase, coef=SIN_C):
    d, s = sine_parts(phase, coef)
    return 1.0 - d, s


def root(x):
    return x * lax.rsqrt(x)


def speeds(turn_x, turn_y):
    sub = lax.broadcasted_iota(I32, turn_x.shape, 0)
    c, s = cos_sin(jnp.where(sub < 4, turn_x, turn_y), SIN_FINE)
    c1 = (2.0 + s * pltpu.roll(s, 4, 0)) * 0.0625
    c2 = (2.0 + c * pltpu.roll(c, 4, 0)) * 0.0625
    return c1 * c1, c2 * c2


def split(x):
    hi = x.astype(BF16)
    return hi, (x - hi.astype(F32)).astype(BF16)


def by_sublane(values, like):
    sub = lax.broadcasted_iota(I32, like.shape, 0)
    out = jnp.full(like.shape, values[0], F32)
    for s in range(1, 8):
        out = jnp.where(sub == s, values[s], out)
    return out


def lanes_of(x, idx):
    return jnp.take_along_axis(x, idx, axis=1)


NT = (((1,), (1,)), ((), ()))


def source_kernel(
    pos_ref, w_ref, os_ref, ranks_ref, tab_ref, turn_c, turn_p,
    out_ref, excl_ref, rank_ref, slot_tile_ref, slot_off_ref, slot_rank_ref, tile_ref,
    w_turned, wave, labels,
):
    step = pl.program_id(0)
    pos = pos_ref[0]
    lane = lax.broadcasted_iota(I32, (8, 128), 1)
    sub = lax.broadcasted_iota(I32, (8, 128), 0)

    @pl.when(step == 0)
    def _():
        ranks = ranks_ref[...].astype(F32)
        owners = os_ref[...].astype(F32)
        rank8 = jnp.zeros((8, 128), F32)
        at_row = []
        for n in range(8):
            e1, e2, half = n // 4, (n // 2) % 2, n % 2
            idx = e1 * 64 + 2 * (lane % 32) + e2
            mine = sub == 4 * half + lane // 32
            at_row.append(
                jnp.sum(jnp.where(mine, lanes_of(owners, idx), 0.0), axis=0, keepdims=True)
            )
            rk = jnp.sum(jnp.where(mine, lanes_of(ranks, idx), 0.0), axis=0, keepdims=True)
            rank8 = jnp.where(sub == n, jnp.broadcast_to(rk, (8, 128)), rank8)
        upto = (
            lax.broadcasted_iota(I32, (128, 128), 0) <= lax.broadcasted_iota(I32, (128, 128), 1)
        )
        upto = jnp.where(upto, 1.0, 0.0).astype(BF16)
        excl8 = jnp.dot(rank8.astype(BF16), upto, preferred_element_type=F32) - rank8
        rank_ref[...] = rank8.astype(I32)
        excl_ref[...] = excl8.astype(I32)
        live = lanes_of(excl8 + rank8, jnp.full((8, 128), 127, I32)).astype(I32)
        n_tiles = (live + 127) >> 7
        first = jnp.zeros((1, 128), I32)
        tile = lane[0:1]
        tile_box, tile_first = jnp.zeros((1, 128), I32), jnp.zeros((1, 128), I32)
        row = lax.broadcasted_iota(I32, (16, 128), 0)
        for n in range(8):
            rk = jnp.broadcast_to(rank8[n : n + 1], (16, 128))
            ahead = jnp.broadcast_to(excl8[n : n + 1], (16, 128)).astype(I32)
            high, low = (ahead >> 6).astype(F32), (ahead & 63).astype(F32)
            label = jnp.where(row == 2, high, jnp.where(row == 3, low, 0.0))
            start = jnp.broadcast_to(first.astype(F32), (16, 128))
            label = jnp.where(row == 0, rk, jnp.where(row == 1, start, label))
            tile_box = jnp.where(tile >= first, n, tile_box)
            tile_first = jnp.where(tile >= first, first, tile_first)
            first = first + n_tiles[n : n + 1]
            labels[:, n * 128 : n * 128 + 128] = label.astype(BF16)
        tile_ref[0:1, :] = tile_box
        tile_ref[1:2, :] = (tile - tile_first) * 128
        tile_ref[2:3, :] = first
        tile_ref[3:8, :] = jnp.zeros((5, 128), I32)
        for j in range(8):
            slot = lax.broadcasted_iota(I32, (128, 128), 0).astype(F32) + j * 128.0
            got = jnp.zeros((16, 128), F32)
            for n in range(8):
                hit = jnp.where(slot == jnp.broadcast_to(at_row[n], (128, 128)), 1.0, 0.0)
                got = got + lax.dot_general(
                    labels[:, n * 128 : n * 128 + 128], hit.astype(BF16), NT,
                    preferred_element_type=F32,
                )
            slot_rank_ref[j : j + 1, :] = got[0:1].astype(I32)
            at = (got[1:2] * 128.0 + got[2:3] * 64.0 + got[3:4]).astype(I32)
            slot_tile_ref[j : j + 1, :] = at >> 7
            slot_off_ref[j : j + 1, :] = at & 127

    corner_xf = (64 * (pos // 4) - 1024).astype(F32)
    h_x = 64 * ((lane % 64) // 8) + 31
    h_y = 64 * (lane % 8) + 31
    h_xf, h_yf = h_x.astype(F32), h_y.astype(F32)
    sq_x, sq_y = speeds(h_xf * (1.0 / 512), h_yf * (1.0 / 512))
    x, y = h_xf * (1.0 / 4096), h_yf * (1.0 / 4096)
    high = lane >= 64

    for box in range(2):
        corner_yf = (64 * ((pos % 4) * 8 + 2 * step + box) - 1024).astype(F32)
        off_y = jnp.where(high, by_sublane(CHILD_OFF[1], lane), by_sublane(CHILD_OFF[0], lane))
        k_y = corner_yf + off_y
        part_y, line_y = sq_y * (k_y * k_y), y * off_y
        for u in range(2):
            for j1 in range(8):
                off_x = CHILD_OFF[u][j1]
                k_x = corner_xf + off_x
                c, s = cos_sin(root(sq_x * (k_x * k_x) + part_y) + (x * off_x + line_y))
                wave[box, 0, (u * 8 + j1) * 8 : (u * 8 + j1) * 8 + 8, :] = c
                wave[box, 1, (u * 8 + j1) * 8 : (u * 8 + j1) * 8 + 8, :] = s
        off_y = by_sublane(PARENT_OFF, lane)
        k_y = corner_yf + off_y
        part_y, line_y = sq_y * (k_y * k_y), y * off_y
        for m in range(4):
            off_x = jnp.where(high, PARENT_OFF[2 * m + 1], PARENT_OFF[2 * m])
            k_x = corner_xf + off_x
            c, s = cos_sin(root(sq_x * (k_x * k_x) + part_y) + (x * off_x + line_y))
            wave[box, 0, 128 + m * 8 : 136 + m * 8, :] = c
            wave[box, 1, 128 + m * 8 : 136 + m * 8, :] = s

        for part in range(4):
            rows = slice(part * 64, part * 64 + 64)
            w_re, w_im = w_ref[0, box, rows, :], w_ref[1, box, rows, :]
            t_re, t_im = turn_c[0, rows, :], turn_c[1, rows, :]
            w_turned[box, 0, rows, :] = w_re * t_re - w_im * t_im
            w_turned[box, 1, rows, :] = w_re * t_im + w_im * t_re

        for e in range(4):
            e1, e2 = e // 2, e % 2
            pick = (2 * (lane // 32) + e1) * 8 + 2 * (lane % 4) + e2
            high_parts = [[], [], [], []]
            low_parts = [[], [], [], []]
            for u in range(2):
                for v in range(2):
                    idx = pick + v * 64
                    for g in range(4):
                        base = (u * 8 + 2 * g) * 8
                        c = jnp.concatenate(
                            [lanes_of(wave[box, 0, base + 8 * i : base + 8 * i + 8, :], idx) for i in (0, 1)]
                        )
                        s = jnp.concatenate(
                            [lanes_of(wave[box, 1, base + 8 * i : base + 8 * i + 8, :], idx) for i in (0, 1)]
                        )
                        at = (u * 2 + v) * 64 + g * 16
                        rows = slice(at, at + 16)
                        for half in range(2):
                            w_re = w_turned[box, 0, rows, half * 128 : half * 128 + 128]
                            w_im = w_turned[box, 1, rows, half * 128 : half * 128 + 128]
                            for z, value in (
                                (half, w_re * c + w_im * s),
                                (2 + half, w_im * c - w_re * s),
                            ):
                                hi, lo = split(value)
                                high_parts[z].append(hi)
                                low_parts[z].append(lo)
            mod_hi = jnp.concatenate([jnp.concatenate(p, axis=0) for p in high_parts], axis=1)
            mod_lo = jnp.concatenate([jnp.concatenate(p, axis=0) for p in low_parts], axis=1)
            first = jnp.dot(tab_ref[...], mod_hi, preferred_element_type=F32)
            second = jnp.dot(tab_ref[0:64, :], mod_lo, preferred_element_type=F32)
            interp = first[0:64] + (first[64:128] + second)
            c = jnp.concatenate(
                [
                    lanes_of(wave[box, 0, 128 + (t // 2) * 8 : 136 + (t // 2) * 8, :], pick + (t % 2) * 64)
                    for t in range(8)
                ]
            )
            s = jnp.concatenate(
                [
                    lanes_of(wave[box, 1, 128 + (t // 2) * 8 : 136 + (t // 2) * 8, :], pick + (t % 2) * 64)
                    for t in range(8)
                ]
            )
            for half in range(2):
                i_re = interp[:, half * 128 : half * 128 + 128]
                i_im = interp[:, half * 128 + 256 : half * 128 + 384]
                t_re = turn_p[0, :, half * 128 : half * 128 + 128]
                t_im = turn_p[1, :, half * 128 : half * 128 + 128]
                g_re = i_re * t_re - i_im * t_im
                g_im = i_re * t_im + i_im * t_re
                out_ref[box, e * 2 + half, 0:64, :] = g_re * c - g_im * s
                out_ref[box, e * 2 + half, 64:128, :] = g_re * s + g_im * c


def source_stage(pos, weights, owner_slot, ranks):
    table = interp_matrix()
    hi = table.astype(jnp.bfloat16)
    lo = (table - hi.astype(np.float32)).astype(jnp.bfloat16)
    stacked = jnp.asarray(np.concatenate([hi, lo], axis=0))
    child = np.array(CHILD_OFF)
    row = np.arange(256)
    off_x = child[row // 128, (row // 8) % 8]
    off_y = child[(row // 64) % 2, row % 8]
    parent = np.array(PARENT_OFF)
    turn_c = jnp.asarray(class_turns(off_x, off_y, -1.0))
    turn_p = jnp.asarray(class_turns(parent[row[:64] // 8], parent[row[:64] % 8], 1.0))

    def whole(*shape):
        return pl.BlockSpec(shape, lambda g, p: (0,) * len(shape))

    return pl.pallas_call(
        source_kernel,
        out_shape=[
            jax.ShapeDtypeStruct((8, 8, 128, 128), F32),
            *[jax.ShapeDtypeStruct((8, 128), I32)] * 6,
        ],
        grid_spec=pltpu.PrefetchScalarGridSpec(
            num_scalar_prefetch=1,
            grid=(4,),
            in_specs=[
                pl.BlockSpec((2, 2, 256, 256), lambda g, p: (0, g, 0, 0)),
                whole(8, 128),
                whole(8, 128),
                whole(128, 256),
                whole(2, 256, 256),
                whole(2, 64, 256),
            ],
            out_specs=[pl.BlockSpec((2, 8, 128, 128), lambda g, p: (g, 0, 0, 0)), *[whole(8, 128)] * 6],
            scratch_shapes=[
                pltpu.VMEM((2, 2, 256, 256), F32),
                pltpu.VMEM((2, 2, 160, 128), F32),
                pltpu.VMEM((16, 1024), BF16),
            ],
        ),
        name="source_stage",
    )(pos, weights, owner_slot, ranks, stacked, turn_c, turn_p)


UNROLL = 16
GROUP = 14
PAIR = 2
MOST_TILES = 96


def target_kernel(
    pos_ref, tile_at, slot_tile, slot_off, delta_hbm, piv_ref, excl_v, rank_v, out_ref,
    delta, pivots, points_x, points_y, edges, sums, box_of, rows_x, parts, lines, tiles, sem,
):
    def fetch(j, b):
        return pltpu.make_async_copy(
            delta_hbm.at[2 * (b % 4) + b // 4, j], delta.at[j, :, b, :], sem.at[j, b]
        )

    for j in range(8):
        for b in range(8):
            fetch(j, b).start()
    pos = pos_ref[0]
    lane = lax.broadcasted_iota(I32, (8, 128), 1)
    sub = lax.broadcasted_iota(I32, (8, 128), 0)
    sub32 = lax.broadcasted_iota(I32, (32, 128), 0).astype(F32)
    corner_x = 64 * (pos >> 2) - 1024
    turn_x = corner_x.astype(F32) * (1.0 / 2048)
    corner_y = (64 * ((pos & 3) * 8 + 2 * (sub & 3) + (sub >> 2)) - 1024).astype(F32)
    turn_y = corner_y * (1.0 / 2048)
    off_col = by_sublane(PARENT_OFF, lane)
    k_x = corner_x.astype(F32) + off_col
    k_sq_x = k_x * k_x

    for h in range(2):
        p = jnp.transpose(piv_ref[:, h, :].astype(F32))
        for g in range(4):
            pivots[h * 4 + g] = p[g * 32 : g * 32 + 32]
    lane32 = lax.broadcasted_iota(I32, (32, 128), 1)

    for j in range(8):
        e1, e2, half = j // 4, (j // 2) % 2, j % 2
        pick = half * 64 + 16 * (lane32 >> 5) + 8 * e1 + ((lane32 & 31) >> 2)
        p = lanes_of(pivots[e2], pick)
        for g in range(1, 4):
            other = lanes_of(pivots[(g >> 1) * 4 + 2 * (g & 1) + e2], pick)
            p = jnp.where((lane32 & 3) == g, other, p)
        p = p.astype(I32)
        box_x = 2 * (half * 4 + (lane32 >> 5)) + e1
        box_y = 2 * (lane32 & 31) + e2
        points_x[j] = (32 * box_x + (p >> 5)).astype(F32)
        points_y[j] = (32 * box_y + (p & 31)).astype(F32)
        start_row = jnp.broadcast_to(excl_v[j : j + 1, :], (8, 128)).astype(F32)
        end_row = start_row + jnp.broadcast_to(rank_v[j : j + 1, :], (8, 128)).astype(F32)
        edges[j, 0:8, :] = lanes_of(end_row, 8 * sub + 7)
        edges[j, 8:16, :] = lanes_of(end_row, 64 + 8 * sub + 7)
        edges[j, 16:24, :] = lanes_of(end_row, jnp.minimum(8 * lane + sub, 127))
        edges[j, 24:32, :] = start_row
    n_all = tile_at[2, 0]

    def one_tile(tile):
        j = tile_at[0, tile]
        row = (tile_at[1, tile] + lane).astype(F32)
        ahead = jnp.where(edges[j, 0:8, :] <= row, 1.0, 0.0)
        ahead = ahead + jnp.where(edges[j, 8:16, :] <= row, 1.0, 0.0)
        group = jnp.minimum(jnp.sum(ahead, axis=0, keepdims=True), 15.0)
        group = jnp.broadcast_to(group, (8, 128))
        inner = jnp.where(lanes_of(edges[j, 16:24, :], group.astype(I32)) <= row, 1.0, 0.0)
        inner = jnp.broadcast_to(jnp.sum(inner, axis=0, keepdims=True), (8, 128))
        idx = jnp.minimum(8.0 * group + inner, 127.0).astype(I32)
        place = row - lanes_of(edges[j, 24:32, :], idx)
        idx32 = jnp.concatenate([idx] * 4)
        mine = sub32 == jnp.concatenate([place] * 4)
        got_x = jnp.where(mine, lanes_of(points_x[j], idx32), 0.0)
        got_y = jnp.where(mine, lanes_of(points_y[j], idx32), 0.0)
        h_x = jnp.broadcast_to(jnp.sum(got_x, axis=0, keepdims=True), (8, 128))
        h_y = jnp.broadcast_to(jnp.sum(got_y, axis=0, keepdims=True), (8, 128))
        sq_x, sq_y = speeds(h_x * (1.0 / 256), h_y * (1.0 / 256))
        x, y = h_x * (1.0 / 2048), h_y * (1.0 / 2048)
        whole_y = wrap(h_y * turn_y)
        part, line = [], []
        for off in PARENT_OFF:
            k_y = corner_y + off
            part.append(sq_y * (k_y * k_y))
            line.append(wrap(whole_y + y * off))
        return idx, sq_x * k_sq_x, wrap(h_x * turn_x) + x * off_col, part, line

    def one_group(i, _):
        at = [jnp.minimum(i * GROUP + h, n_all - 1) for h in range(GROUP)]
        found = [one_tile(tile) for tile in at]
        for tile, (idx, part_x, line_x, part, line) in zip(at, found):
            box_of[tile] = idx
            rows_x[tile, 0:8, :] = part_x
            rows_x[tile, 8:16, :] = line_x
            for t2 in range(8):
                parts[tile, t2] = part[t2]
                lines[tile, t2] = line[t2]
        return 0

    lax.fori_loop(0, (n_all + GROUP - 1) // GROUP, one_group, 0)

    def one_total(j, _):
        for b in range(8):
            fetch(j, b).wait()
        total_re = jnp.zeros((8, 128), F32)
        total_im = jnp.zeros((8, 128), F32)
        for t in range(64):
            total_re = total_re + delta[j, t]
            total_im = total_im + delta[j, 64 + t]
        sums[j, 0:8, :] = total_re
        sums[j, 8:16, :] = total_im
        return 0

    lax.fori_loop(0, 8, one_total, 0)

    def one_sum(tile):
        j = tile_at[0, tile]
        idx = box_of[tile]
        acc_re = lanes_of(sums[j, 0:8, :], idx)
        acc_im = lanes_of(sums[j, 8:16, :], idx)
        for t1 in range(8):
            part_x = jnp.broadcast_to(rows_x[tile, t1 : t1 + 1, :], (8, 128))
            line_x = jnp.broadcast_to(rows_x[tile, 8 + t1 : 9 + t1, :], (8, 128))
            for t2 in range(8):
                t = t1 * 8 + t2
                d_re = lanes_of(delta[j, t], idx)
                d_im = lanes_of(delta[j, 64 + t], idx)
                d, s = sine_parts(
                    root(part_x + parts[tile, t2]) + (line_x + lines[tile, t2]), SIN_C
                )
                acc_re = acc_re - (d * d_re + s * d_im)
                acc_im = acc_im + (s * d_re - d * d_im)
        acc_re = acc_re + pltpu.roll(acc_re, 4, 0)
        acc_im = acc_im + pltpu.roll(acc_im, 4, 0)
        return jnp.where(sub < 4, acc_re, acc_im)

    def one_pair(i, _):
        at = [jnp.minimum(i * PAIR + h, n_all - 1) for h in range(PAIR)]
        done = [one_sum(tile) for tile in at]
        for tile, value in zip(at, done):
            tiles[tile] = value
        return 0

    lax.fori_loop(0, (n_all + PAIR - 1) // PAIR, one_pair, 0)

    def one_owner(o, _):
        for part in range(2):
            out = jnp.zeros((8, 128), F32)
            for q in range(4):
                tile = slot_tile[o * 8 + part * 4 + q]
                off = slot_off[o * 8 + part * 4 + q]
                joined = jnp.where(lane >= off, tiles[tile], tiles[tile + 1])
                joined = pltpu.roll(joined, (q * 32 + 128 - off) & 127, 1)
                out = joined if q == 0 else jnp.where((lane >> 5) == q, joined, out)
            out_ref[o, :, part * 128 : part * 128 + 128] = out
        return 0

    lax.fori_loop(0, 128, one_owner, 0, unroll=UNROLL)


def target_stage(pos, excl, rank, slot_tile, slot_off, tile_at, delta, piv):
    smem = pl.BlockSpec(memory_space=pltpu.SMEM)
    vmem = pl.BlockSpec(memory_space=pltpu.VMEM)
    hbm = pl.BlockSpec(memory_space=pl.ANY)
    return pl.pallas_call(
        target_kernel,
        out_shape=pltpu.VMEM((128, 8, 256), F32),
        in_specs=[smem, smem, smem, smem, hbm, vmem, vmem, vmem],
        out_specs=vmem,
        scratch_shapes=[
            pltpu.VMEM((8, 128, 8, 128), F32),
            pltpu.VMEM((8, 32, 128), F32),
            pltpu.VMEM((8, 32, 128), F32),
            pltpu.VMEM((8, 32, 128), F32),
            pltpu.VMEM((8, 32, 128), F32),
            pltpu.VMEM((8, 16, 128), F32),
            pltpu.VMEM((MOST_TILES, 8, 128), I32),
            pltpu.VMEM((MOST_TILES, 16, 128), F32),
            pltpu.VMEM((MOST_TILES, 8, 8, 128), F32),
            pltpu.VMEM((MOST_TILES, 8, 8, 128), F32),
            pltpu.VMEM((MOST_TILES, 8, 128), F32),
            pltpu.SemaphoreType.DMA((8, 8)),
        ],
        name="target_stage",
    )(
        pos, tile_at, slot_tile.reshape(1024), slot_off.reshape(1024), delta, piv, excl, rank
    )


def owner_kernel(pos_ref, rank_ref, in_ref, out_ref, gathered):
    pos = pos_ref[0]
    sub = lax.broadcasted_iota(I32, (8, 256), 0)
    for p1 in range(16):
        part = [in_ref[p1 * 8 + q] + in_ref[p1 * 8 + 4 + q] for q in range(4)]
        for m in range(2):
            even, odd = part[2 * m], part[2 * m + 1]
            row = p1 * 16 + m * 8
            gathered[0, row : row + 8, :] = jnp.where(sub < 4, even, pltpu.roll(odd, 4, 0))
            gathered[1, row : row + 8, :] = jnp.where(sub < 4, pltpu.roll(even, 4, 0), odd)
    i = lax.broadcasted_iota(I32, (32, 256), 0)
    for z in range(2):
        rows = jnp.transpose(gathered[z])
        for k in range(8):
            live = i < rank_ref[pos >> 4, (pos & 15) * 8 + k]
            out_ref[z, :, k, :] = jnp.where(live, rows[k * 32 : k * 32 + 32], 0.0)


def owner_stage(pos, rank, received):
    smem = pl.BlockSpec(memory_space=pltpu.SMEM)
    vmem = pl.BlockSpec(memory_space=pltpu.VMEM)
    return pl.pallas_call(
        owner_kernel,
        out_shape=jax.ShapeDtypeStruct((2, 32, 8, 256), F32),
        in_specs=[smem, smem, vmem],
        out_specs=vmem,
        scratch_shapes=[pltpu.VMEM((2, 256, 256), F32)],
        name="owner_stage",
    )(pos, rank, received)


def local(child_weights, pivots, ranks, owner_slot):
    pos = lax.axis_index("grp") * lax.axis_size("dev") + lax.axis_index("dev")
    pos = pos.astype(I32).reshape(1)
    spread = jnp.broadcast_to(pivots.reshape(1, 2, 128), (128, 2, 128))
    all_pivots = lax.all_to_all(spread, AXES, split_axis=0, concat_axis=0, tiled=True)
    at = owner_slot.reshape(8, 128)
    weights = child_weights.reshape(2, 8, 256, 256)
    delta, excl, rank, slot_tile, slot_off, slot_rank, tile_at = source_stage(
        pos, weights, at, ranks.reshape(8, 128)
    )
    all_pivots = pltpu.with_memory_space_constraint(all_pivots, pltpu.VMEM)
    send = target_stage(pos, excl, rank, slot_tile, slot_off, tile_at, delta, all_pivots)
    received = lax.all_to_all(send, AXES, split_axis=0, concat_axis=0, tiled=True)
    received = pltpu.with_memory_space_constraint(received, pltpu.VMEM)
    return owner_stage(pos, slot_rank, received)


def solution(mesh):
    in_specs = (P(None, AXES, None, None, None), P(AXES, None), P(), P())
    out_specs = P(None, None, AXES, None)
    return jax.shard_map(local, mesh=mesh, in_specs=in_specs, out_specs=out_specs, check_vma=False)
```
